32 devices in a mesh: groups: 2 (over y), space: 4 (over z), tm: 2 (over x), freq: 2 (over core).
Axes of the slice: x: 2, y: 2, z: 4, core: 2. Of those that a mesh axis runs over, the one named last changes fastest.
Arguments:
- snapshots: float32 [16, 64, 16384], P(None, 'space', ('groups', 'tm')), parts along dimension 2, may hold values from -28 to 28, as said below
- weights: float32 [16384], P(('groups', 'tm', 'space')), parts along dimension 0, may hold values from 0.3 to 3
Outputs:
- modes: float32 [16, 2, 16, 16384], P('freq', None, None, ('groups', 'tm', 'space')), parts along dimension 3
- r_factor: float32 [4, 16, 16, 16], P('groups', 'freq'), parts along dimension 0
The draws below stay inside these ranges and needn't reach their ends.
There are 2 independent parts, one for each index of `groups`. The reference program is written for one: setup_inputs(seed, part) draws one part's arguments, and reference() takes and returns one part's arrays. A program takes and returns all parts, laid end to end along the dimension named above; each array names one. Nothing has to cross between parts.
Inputs may be any that keep to these rules, and one draw needn't show every extreme that they name: `snapshots`: velocity fluctuations of the jet.
All inputs are finite; a program needn't handle non-finite values.
Results may differ from the reference program's by a relative error of at most 0.00009.
Values sent between devices are 32-bit elements; how exact they have to be, the bound alone decides.
A program may use at most 64 MiB of HBM per device.

```python
import math
import jax
import jax.numpy as jnp
from jax import lax

NB = 16
SEGMENT_FRAMES = 64
NF = 16
M = 8192


def draw_snapshots(key, part):
    first_key = jax.random.fold_in(jax.random.fold_in(key, 11), 0)
    place = jnp.arange(M, dtype=jnp.float32) / M
    envelope = 3.0 ** place
    field = jnp.clip(jax.random.normal(first_key, (NB, SEGMENT_FRAMES, M), jnp.float32), -6.0, 6.0)
    return field * envelope[None, None, :]


def levels(rng, extent, cuts, smallest, largest):
    factor_of, own = 1.0, jax.random.fold_in(rng, 6)
    for dim, blocks in cuts:
        heights = jnp.exp(jax.random.uniform(jax.random.fold_in(own, dim), (blocks,), jnp.float32, smallest / len(cuts), largest / len(cuts)))
        factor_of = factor_of * jnp.repeat(heights, extent[dim] // blocks).reshape([-1 if axis == dim else 1 for axis in range(len(extent))])
    return factor_of


def setup_inputs(seed: int = 0, part: int = 0) -> dict:
    seeds = jax.random.split(jax.random.key(seed), 3)
    part_splits = jax.random.split(jax.random.fold_in(seeds[2], part), 3)
    return {
        "snapshots": draw_snapshots(jax.random.fold_in(jax.random.fold_in(seeds[2], part), 71), part),
        "weights": jnp.clip(jnp.exp(math.log(3.0) - 2.3025851 * jax.random.uniform(part_splits[1], (M,), jnp.float32) ** levels(part_splits[1], (M,), ((0, 8),), -0.2, 0.2)), 0.3, 3.0),
    }


epsilon = 1e-05

def dft_table(first_freq, how_many, initial_moment, elapsed_timespan):
    recorded_moments = initial_moment + jnp.arange(elapsed_timespan, dtype=jnp.int32)
    fourier_cycle_rate = first_freq + 1 + jnp.arange(how_many, dtype=jnp.int32)
    every_time = jnp.arange(SEGMENT_FRAMES, dtype=jnp.float32)
    tapers = 0.5 - 0.5 * jnp.cos(2.0 * jnp.pi * every_time / SEGMENT_FRAMES)
    norm_taper = jnp.sqrt(jnp.sum(tapers * tapers))
    segment_hann_weighting = 0.5 - 0.5 * jnp.cos(2.0 * jnp.pi * recorded_moments.astype(jnp.float32) / SEGMENT_FRAMES)
    weighted = segment_hann_weighting / norm_taper
    twiddle_angle_list = fourier_cycle_rate[:, None] * recorded_moments[None, :] % SEGMENT_FRAMES
    phases = 2.0 * jnp.pi * twiddle_angle_list.astype(jnp.float32) / SEGMENT_FRAMES
    paired = jnp.stack([jnp.cos(phases) * weighted[None, :], -jnp.sin(phases) * weighted[None, :]], axis=1)
    return paired.reshape(2 * how_many, elapsed_timespan)

def contract(left, right):
    return jnp.einsum('fbm,fcm->fbc', left, right, precision=lax.Precision.HIGHEST)

def gram_terms(spectra, weights):
    real_part = spectra[:, 0]
    imag_part = spectra[:, 1]
    weighted_re = real_part * weights
    weighted_im = imag_part * weights
    gram_re = contract(weighted_re, real_part) + contract(weighted_im, imag_part)
    gram_im = contract(weighted_re, imag_part) - contract(weighted_im, real_part)
    return jnp.stack([gram_re, gram_im])

def factor(gram):
    positions = jnp.arange(NB, dtype=jnp.int32)
    rows_re = []
    rows_im = []
    for i in range(NB):
        accum_re = gram[0][:, i, :]
        accum_im = gram[1][:, i, :]
        for p in range(i):
            left_re = rows_re[p][:, i][:, None]
            left_im = rows_im[p][:, i][:, None]
            accum_re = accum_re - (left_re * rows_re[p] + left_im * rows_im[p])
            accum_im = accum_im - (left_re * rows_im[p] - left_im * rows_re[p])
        pivot = jnp.sqrt(accum_re[:, i] + epsilon)
        beyond = (positions > i)[None, :]
        at_diag = (positions == i)[None, :]
        rows_re.append(jnp.where(beyond, accum_re / pivot[:, None], 0.0) + jnp.where(at_diag, pivot[:, None], 0.0))
        rows_im.append(jnp.where(beyond, accum_im / pivot[:, None], 0.0))
    upper_re = jnp.stack(rows_re, axis=1)
    upper_im = jnp.stack(rows_im, axis=1)
    inverse_re = [None] * NB
    inverse_im = [None] * NB
    for i in range(NB - 1, -1, -1):
        accum_re = jnp.broadcast_to(jnp.where(positions == i, 1.0, 0.0).astype(jnp.float32)[None, :], upper_re[:, 0, :].shape)
        accum_im = jnp.zeros_like(accum_re)
        for p in range(i + 1, NB):
            coef_re = upper_re[:, i, p][:, None]
            coef_im = upper_im[:, i, p][:, None]
            accum_re = accum_re - (coef_re * inverse_re[p] - coef_im * inverse_im[p])
            accum_im = accum_im - (coef_re * inverse_im[p] + coef_im * inverse_re[p])
        pivot = upper_re[:, i, i][:, None]
        inverse_re[i] = accum_re / pivot
        inverse_im[i] = accum_im / pivot
    return (upper_re, upper_im, jnp.stack(inverse_re, axis=1), jnp.stack(inverse_im, axis=1))

def apply_inverse(left, inverse):
    return jnp.einsum('fbm,fbc->fcm', left, inverse, precision=lax.Precision.HIGHEST)

def build_modes(spectra, inverse_re, inverse_im):
    real_part = spectra[:, 0]
    imag_part = spectra[:, 1]
    modes_re = apply_inverse(real_part, inverse_re) - apply_inverse(imag_part, inverse_im)
    modes_im = apply_inverse(real_part, inverse_im) + apply_inverse(imag_part, inverse_re)
    return jnp.stack([modes_re, modes_im], axis=1)

def reference(snapshots, weights):
    table = dft_table(0, NF, 0, SEGMENT_FRAMES)
    spectra = jnp.einsum('ft,btm->fbm', table, snapshots, precision=lax.Precision.HIGHEST)
    spectra = spectra.reshape(NF, 2, NB, M)
    gram = gram_terms(spectra, weights) / M
    upper_re, upper_im, inverse_re, inverse_im = factor(gram)
    modes = build_modes(spectra, inverse_re, inverse_im)
    return (modes, jnp.stack([upper_re, upper_im]))
```

```python
import functools

import jax
import jax.numpy as jnp
import numpy as np
from jax import lax
from jax.experimental import pallas as pl
from jax.experimental.pallas import tpu as pltpu
from jax.sharding import PartitionSpec as P

SEGMENT_FRAMES = 64
NF = 16
GROUP = 4
LANES = 128

epsilon = 1e-05
MESH = pl.DeviceIdType.MESH
HIGHEST = lax.Precision.HIGHEST


def dft_table(half, senders, local_times):
    moments = np.arange(SEGMENT_FRAMES)
    hann = 0.5 - 0.5 * np.cos(2.0 * np.pi * moments / SEGMENT_FRAMES)
    taper = hann / np.sqrt(np.sum(hann * hann))
    angle = (np.arange(NF) + 1)[:, None] * moments[None, :] % SEGMENT_FRAMES
    phase = 2.0 * np.pi * angle / SEGMENT_FRAMES
    pair = np.stack([np.cos(phase) * taper, -np.sin(phase) * taper])
    pair = pair.reshape(2, NF // half, half, senders, local_times)
    full = np.einsum("rhfzt,bc->hrbfzct", pair, np.eye(GROUP))
    shape = (2 * NF * GROUP, senders * GROUP * local_times)
    return full.reshape(shape).astype(np.float32)


def xor(a, d, bits):
    out = 0
    for k in range(bits):
        first = lax.rem(lax.div(a, 1 << k), 2)
        second = (d >> k) & 1
        out = out + (1 << k) * (first + second - 2 * first * second)
    return out


def peers_along(me, count):
    bits = count.bit_length() - 1
    if count != 1 << bits:
        return [lax.rem(me + d, count) for d in range(1, count)]
    far = list(range(count // 2, count))
    return [xor(me, d, bits) for d in far + list(range(1, count // 2))]


def spectra_kernel(
    exchange, space, tm, total, snap, weight_in, table_in, x_out, g_out,
    weight, table, recv, spec, inbox, acc, g_send, g_recv,
    c_sem, s_send, s_recv, l_sem, p_send, p_recv, gs_sem, gr_sem,
):
    core = lax.axis_index("freq")
    z = lax.axis_index("space")
    m = lax.axis_index("tm")
    other = 1 - core
    nb, rows = recv.shape[1], recv.shape[3]
    width = min(rows, LANES)
    chunks = rows // width
    half = NF // 2
    n = nb * half
    z_peers = peers_along(z, space)
    m_peers = peers_along(m, tm)
    near = [(m, p) for p in z_peers]
    away = [(o, p) for o in m_peers for p in [*z_peers, z]]
    g_peers = []
    for o, p in away + near:
        g_peers += [(other, o, p), (core, o, p)]
    g_peers.append((other, m, z))

    def at(c, o, p):
        return {"freq": c, "tm": o, "space": p}

    def number(c, o, p):
        return (c * tm + o) * space + p

    def cols(q):
        return pl.ds(q * width, width)

    def source(p, q):
        start = (p * 2 + core) * rows + q * width
        return snap.at[:, :, pl.ds(pl.multiple_of(start, width), width)]

    def local(q):
        if exchange:
            return pltpu.make_async_copy(
                source(z, q), recv.at[z, :, :, cols(q)], l_sem.at[q]
            )
        return pltpu.make_async_copy(
            snap.at[:, :, cols(q)], recv.at[0, :, :, cols(q)], l_sem.at[q]
        )

    def send(q, i):
        return pltpu.make_async_remote_copy(
            src_ref=source(z_peers[i], q),
            dst_ref=recv.at[z, :, :, cols(q)],
            send_sem=s_send.at[q, i],
            recv_sem=s_recv.at[q, z],
            device_id={"space": z_peers[i]},
            device_id_type=MESH,
        )

    def arrive(q, i):
        p = z_peers[i]
        return pltpu.make_async_remote_copy(
            src_ref=source(p, q),
            dst_ref=recv.at[p, :, :, cols(q)],
            send_sem=s_send.at[q, i],
            recv_sem=s_recv.at[q, p],
            device_id={"space": p},
            device_id_type=MESH,
        )

    def trade(q):
        return pltpu.make_async_remote_copy(
            src_ref=spec.at[q, other],
            dst_ref=inbox.at[q],
            send_sem=p_send.at[q],
            recv_sem=p_recv.at[q],
            device_id={"freq": other},
            device_id_type=MESH,
        )

    def gram_copy(i, slot):
        c, o, p = g_peers[i]
        return pltpu.make_async_remote_copy(
            src_ref=g_send.at[c],
            dst_ref=g_recv.at[slot],
            send_sem=gs_sem.at[i],
            recv_sem=gr_sem.at[slot],
            device_id=at(c, o, p),
            device_id_type=MESH,
        )

    barrier = pltpu.get_barrier_semaphore()
    for peer in g_peers:
        pl.semaphore_signal(barrier, inc=1, device_id=at(*peer), device_id_type=MESH)
    constants = [
        pltpu.make_async_copy(weight_in, weight, c_sem.at[0]),
        pltpu.make_async_copy(table_in, table, c_sem.at[1]),
    ]
    for copy in constants:
        copy.start()
    pl.semaphore_wait(barrier, len(g_peers))

    hops = range(len(z_peers)) if exchange else range(0)
    for q in range(chunks):
        for i in hops:
            send(q, i).start()
    for q in range(chunks):
        local(q).start()
    for copy in constants:
        copy.wait()

    for q in range(chunks):
        local(q).wait()
        for i in hops:
            arrive(q, i).wait_recv()
        flat = [
            recv[:, b : b + GROUP, :, q * width : (q + 1) * width].reshape(-1, width)
            for b in range(0, nb, GROUP)
        ]
        got = jnp.dot(
            table[...], jnp.concatenate(flat, axis=1),
            precision=HIGHEST, preferred_element_type=jnp.float32,
        )
        step = GROUP * half
        w = weight[core, :, q * width : (q + 1) * width]
        for c in range(2):
            pair = []
            for r in range(2):
                top = (c * 2 + r) * step
                pair.append(
                    jnp.concatenate(
                        [
                            got[top : top + step, g * width : (g + 1) * width]
                            for g in range(nb // GROUP)
                        ],
                        axis=0,
                    )
                )
                spec[q, c, r] = pair[r]
            re, im = pair
            left = jnp.concatenate([re * w, im * w], axis=1)
            right = jnp.concatenate([re + im, im - re], axis=1)
            product = lax.dot_general(
                left, right, (((1,), (1,)), ((), ())),
                precision=HIGHEST, preferred_element_type=jnp.float32,
            )
            acc[c] = product if q == 0 else acc[c] + product
        if q < chunks - 1:
            trade(q).start()

    lane = lax.broadcasted_iota(jnp.int32, (nb, n), 1)
    for c in range(2):
        out = acc[c, pl.ds(0, nb, stride=half), :]
        for f in range(1, half):
            out = jnp.where(
                lane % half == f, acc[c, pl.ds(f, nb, stride=half), :], out
            )
        g_send[c] = out
    mine = number(core, m, z)
    for i in range(len(g_peers)):
        gram_copy(i, mine).start()
    trade(chunks - 1).start()
    g_recv[mine] = g_send[core]

    def put(ref, q, start):
        place = pl.ds(pl.multiple_of(start * rows + q * width, width), width)
        for r in range(2):
            for f in range(half):
                first = r * n + f * nb
                x_out[first : first + nb, place] = ref[r, pl.ds(f, nb, stride=half), :]

    for q in range(chunks):
        put(spec.at[q, core], q, core)
    for q in range(chunks):
        trade(q).wait_recv()
        put(inbox.at[q], q, other)
    for q in range(chunks):
        trade(q).wait_send()
        for i in hops:
            send(q, i).wait_send()
    for i, peer in enumerate(g_peers):
        gram_copy(i, number(*peer)).wait_recv()
    for i in range(len(g_peers)):
        gram_copy(i, mine).wait_send()
    slots = [g_recv[s] for s in range(2 * space * tm)]
    while len(slots) > 1:
        slots = [
            sum(slots[i + 1 : i + 2], slots[i]) for i in range(0, len(slots), 2)
        ]
    g_out[...] = slots[0] * (1.0 / total)


def modes_kernel(half, gram, x, modes, upper):
    nb, lanes = gram.shape
    row = lax.broadcasted_iota(jnp.int32, (nb, lanes), 0)
    lane = lax.broadcasted_iota(jnp.int32, (nb, lanes), 1)
    col = lane % nb
    which = lane // nb

    def pick(a, index):
        return jnp.take_along_axis(a, index, axis=1, mode="promise_in_bounds")

    mixed = pick(gram[...], col * half + which)
    turned = mixed.T
    turned = jnp.concatenate(
        [turned[f * nb : (f + 1) * nb] for f in range(half)], axis=1
    )
    re = (mixed + turned) * 0.5 + jnp.where(row == col, epsilon, 0.0)
    im = (mixed - turned) * 0.5
    diag = jnp.zeros_like(re)
    for p in range(nb):
        index = which * nb + p
        cr, ci = pick(re, index), pick(im, index)
        diag = jnp.where(row == p, cr, diag)
        if p == nb - 1:
            break
        inv = 1.0 / cr[p : p + 1]
        mr, mi = cr * inv, ci * inv
        pr, pi = re[p : p + 1], im[p : p + 1]
        here = col == p
        nr = jnp.where(here, 0.0, re) - (
            mr * jnp.where(here[:1], 1.0, pr) - mi * jnp.where(here[:1], 0.0, pi)
        )
        ni = jnp.where(here, 0.0, im) - (
            mr * jnp.where(here[:1], 0.0, pi) + mi * jnp.where(here[:1], 1.0, pr)
        )
        re = jnp.where(row > p, nr, re)
        im = jnp.where(row > p, ni, im)
    pivot = jnp.sqrt(diag)
    scale = 1.0 / pivot
    re, im = re * scale, im * scale
    ur = jnp.where(col > row, re, jnp.where(col == row, pivot, 0.0))
    ui = jnp.where(col > row, im, 0.0)
    lr = jnp.where(col < row, re, jnp.where(col == row, scale, 0.0))
    li = jnp.where(col < row, im, 0.0)
    for f in range(half):
        upper[0, f] = ur[:, f * nb : (f + 1) * nb]
        upper[1, f] = ui[:, f * nb : (f + 1) * nb]
    parts = []
    for f in range(half):
        fr = jnp.where(which == f, lr, 0.0)
        fi = jnp.where(which == f, li, 0.0)
        parts.append(jnp.concatenate([fr, fi], axis=1))
        parts.append(jnp.concatenate([-fi, fr], axis=1))
    big = jnp.concatenate(parts, axis=0)
    out = jnp.dot(big, x[...], precision=HIGHEST, preferred_element_type=jnp.float32)
    modes[...] = out.reshape(modes.shape)


def in_hbm(a):
    return pltpu.with_memory_space_constraint(a, pltpu.HBM)


def on_device(snapshots, weights):
    freq = lax.axis_size("freq")
    space = lax.axis_size("space")
    tm = lax.axis_size("tm")
    assert freq == 2
    half = NF // freq
    nb, local_times, columns = snapshots.shape
    rows = columns // (space * freq)
    exchange = local_times % 8 == 0
    if not exchange:
        shaped = snapshots.reshape(nb, local_times, space, freq, rows)
        own = lax.dynamic_index_in_dim(shaped, lax.axis_index("freq"), 3, keepdims=False)
        pieces = lax.all_to_all(own, "space", split_axis=2, concat_axis=1, tiled=True)
        snapshots = pieces.reshape(nb, SEGMENT_FRAMES, rows)
    senders = space if exchange else 1
    times = SEGMENT_FRAMES // senders
    chunks = rows // min(rows, LANES)
    table = jnp.asarray(dft_table(half, senders, times))
    weight = weights.reshape(freq, 1, rows)
    lanes = nb * half
    peers = freq * space * tm
    vmem = pl.BlockSpec(memory_space=pltpu.VMEM)
    dma = pltpu.SemaphoreType.DMA
    x, gram = pl.pallas_call(
        functools.partial(
            spectra_kernel, exchange, space, tm, weights.shape[0] * space * tm
        ),
        out_shape=(
            pltpu.VMEM((2 * lanes, freq * rows), jnp.float32),
            pltpu.VMEM((nb, lanes), jnp.float32),
        ),
        in_specs=[pl.BlockSpec(memory_space=pltpu.HBM)] * 3,
        out_specs=(vmem, vmem),
        scratch_shapes=[
            pltpu.VMEM(weight.shape, jnp.float32),
            pltpu.VMEM(table.shape, jnp.float32),
            pltpu.VMEM((senders, nb, times, rows), jnp.float32),
            pltpu.VMEM((chunks, freq, 2, lanes, rows // chunks), jnp.float32),
            pltpu.VMEM((chunks, 2, lanes, rows // chunks), jnp.float32),
            pltpu.VMEM((freq, lanes, lanes), jnp.float32),
            pltpu.VMEM((freq, nb, lanes), jnp.float32),
            pltpu.VMEM((peers, nb, lanes), jnp.float32),
            dma((2,)),
            dma((chunks, max(space - 1, 1))),
            dma((chunks, space)),
            dma((chunks,)),
            dma((chunks,)),
            dma((chunks,)),
            dma((peers,)),
            dma((peers,)),
        ],
        compiler_params=pltpu.CompilerParams(
            collective_id=0, has_side_effects=True, vmem_limit_bytes=52 * 2**20
        ),
        name="spectra",
    )(snapshots, in_hbm(weight), in_hbm(table))
    modes, upper = pl.pallas_call(
        functools.partial(modes_kernel, half),
        out_shape=(
            jax.ShapeDtypeStruct((half, 2, nb, freq * rows), jnp.float32),
            jax.ShapeDtypeStruct((2, half, nb, nb), jnp.float32),
        ),
        in_specs=[vmem, vmem],
        out_specs=(vmem, vmem),
        compiler_params=pltpu.CompilerParams(vmem_limit_bytes=40 * 2**20),
        name="modes",
    )(gram, x)
    return modes, upper


def solution(mesh):
    return jax.shard_map(
        on_device,
        mesh=mesh,
        in_specs=(P(None, "space", ("groups", "tm")), P(("groups", "tm", "space"))),
        out_specs=(
            P("freq", None, None, ("groups", "tm", "space")),
            P("groups", "freq", None, None),
        ),
        check_vma=False,
    )
```

```python
import functools

import jax
import jax.numpy as jnp
import numpy as np
from jax import lax
from jax.experimental import pallas as pl
from jax.experimental.pallas import tpu as pltpu
from jax.sharding import PartitionSpec as P

SEGMENT_FRAMES = 64
NF = 16
GROUP = 4
LANES = 128

epsilon = 1e-05
MESH = pl.DeviceIdType.MESH
HIGHEST = lax.Precision.HIGHEST


def dft_table(half, senders, local_times):
    moments = np.arange(SEGMENT_FRAMES)
    hann = 0.5 - 0.5 * np.cos(2.0 * np.pi * moments / SEGMENT_FRAMES)
    taper = hann / np.sqrt(np.sum(hann * hann))
    angle = (np.arange(NF) + 1)[:, None] * moments[None, :] % SEGMENT_FRAMES
    phase = 2.0 * np.pi * angle / SEGMENT_FRAMES
    pair = np.stack([np.cos(phase) * taper, -np.sin(phase) * taper])
    pair = pair.reshape(2, NF // half, half, senders, local_times)
    full = np.einsum("rhfzt,bc->hrbfzct", pair, np.eye(GROUP))
    shape = (2 * NF * GROUP, senders * GROUP * local_times)
    return full.reshape(shape).astype(np.float32)


def send_order(k, space, chunks):
    middle = space // 2
    halves = [p for p in range(middle)], [p for p in range(middle, space)]
    here, there = halves if k < middle else halves[::-1]
    cross = sorted(there, key=lambda p: -abs(p - k))
    near = [p for p in here if p != k]
    early, late = cross[:-1], cross[-1:]
    order = [(0, p) for p in late]
    if k in (middle - 1, middle):
        order += [(q, p) for q in range(chunks) for p in early]
        order += [(q, p) for q in range(chunks) for p in near + late]
    else:
        order += [(q, p) for q in range(chunks) for p in early + near]
        order += [(q, p) for q in range(chunks) for p in late]
    return list(dict.fromkeys(order))


def spectra_kernel(
    exchange, space, tm, total, snap, weight_in, table_in, x_out, g_out,
    weight, table, recv, spec, inbox, acc, g_send, g_recv,
    c_sem, s_send, s_recv, p_send, p_recv, g_sent, g_got, here, ready,
):
    core = lax.axis_index("freq")
    z = lax.axis_index("space")
    m = lax.axis_index("tm")
    other = 1 - core
    nb, rows = recv.shape[1], recv.shape[3]
    width = min(rows, LANES)
    chunks = rows // width
    half = NF // 2
    n = nb * half
    lines = [(c, lax.rem(m + d, tm)) for d in range(tm) for c in (core, other)][1:]

    mine = (core * tm + m) * space + z

    def cols(q):
        return pl.ds(q * width, width)

    def source(p, q):
        start = (p * 2 + core) * rows + q * width
        return snap.at[:, :, pl.ds(pl.multiple_of(start, width), width)]

    def local(q):
        return pltpu.make_async_copy(
            source(z, q) if exchange else snap.at[:, :, cols(q)],
            recv.at[z if exchange else 0, :, :, cols(q)],
            s_recv.at[q],
        )

    def send(q, p):
        return pltpu.make_async_remote_copy(
            src_ref=source(p, q),
            dst_ref=recv.at[z, :, :, cols(q)],
            send_sem=s_send,
            recv_sem=s_recv.at[q],
            device_id={"space": p},
            device_id_type=MESH,
        )

    def wait(ref, semaphore):
        pltpu.make_async_copy(ref, ref, semaphore).wait()

    def trade(q):
        return pltpu.make_async_remote_copy(
            src_ref=spec.at[q, other],
            dst_ref=inbox.at[q],
            send_sem=p_send,
            recv_sem=p_recv,
            device_id={"freq": other},
            device_id_type=MESH,
        )

    def gram_copy(c, o, p):
        return pltpu.make_async_remote_copy(
            src_ref=g_send.at[c],
            dst_ref=g_recv.at[mine],
            send_sem=g_sent,
            recv_sem=g_got,
            device_id={"freq": c, "tm": o, "space": p},
            device_id_type=MESH,
        )

    def greet(semaphore, **place):
        pl.semaphore_signal(
            semaphore, inc=1, device_id=place, device_id_type=MESH
        )

    barrier = pltpu.get_barrier_semaphore()
    for p in range(1, space):
        @pl.when(z < p)
        def _():
            greet(barrier, space=p)

    @pl.when(z > 0)
    def _():
        pl.semaphore_wait(barrier, z)

    for p in range(space - 1):
        @pl.when(z > p)
        def _():
            greet(here.at[z], space=p)

    for k in range(space):
        @pl.when(z == k)
        def _():
            met = set(range(k + 1))
            for q, p in send_order(k, space, chunks) if exchange else ():
                if p not in met:
                    pl.semaphore_wait(here.at[p], 1)
                    met.add(p)
                send(q, p).start()
            for p in range(space):
                if p not in met:
                    pl.semaphore_wait(here.at[p], 1)

    constants = [
        pltpu.make_async_copy(weight_in, weight, c_sem.at[0]),
        pltpu.make_async_copy(table_in, table, c_sem.at[1]),
    ]
    for copy in constants:
        copy.start()
    for q in range(chunks):
        local(q).start()

    @pl.when(z == 0)
    def _():
        for c, o in lines:
            greet(barrier, freq=c, tm=o)
        pl.semaphore_wait(barrier, len(lines))
        for p in range(1, space):
            greet(ready, space=p)

    @pl.when(z > 0)
    def _():
        pl.semaphore_wait(ready, 1)

    for copy in constants:
        copy.wait()

    for q in range(chunks):
        wait(recv.at[:, :, :, cols(q)], s_recv.at[q])
        flat = [
            recv[:, b : b + GROUP, :, q * width : (q + 1) * width].reshape(-1, width)
            for b in range(0, nb, GROUP)
        ]
        got = jnp.dot(
            table[...], jnp.concatenate(flat, axis=1),
            precision=HIGHEST, preferred_element_type=jnp.float32,
        )
        step = GROUP * half
        w = weight[core, :, q * width : (q + 1) * width]
        for c in range(2):
            pair = []
            for r in range(2):
                top = (c * 2 + r) * step
                pair.append(
                    jnp.concatenate(
                        [
                            got[top : top + step, g * width : (g + 1) * width]
                            for g in range(nb // GROUP)
                        ],
                        axis=0,
                    )
                )
                spec[q, c, r] = pair[r]
            re, im = pair
            left = jnp.concatenate([re * w, im * w], axis=1)
            right = jnp.concatenate([re + im, im - re], axis=1)
            product = lax.dot_general(
                left, right, (((1,), (1,)), ((), ())),
                precision=HIGHEST, preferred_element_type=jnp.float32,
            )
            acc[c] = product if q == 0 else acc[c] + product
        if q < chunks - 1:
            trade(q).start()

    lane = lax.broadcasted_iota(jnp.int32, (nb, n), 1)
    for c in range(2):
        out = acc[c, pl.ds(0, nb, stride=half), :]
        for f in range(1, half):
            out = jnp.where(
                lane % half == f, acc[c, pl.ds(f, nb, stride=half), :], out
            )
        g_send[c] = out
    for p in range(space):
        for c, o in lines:
            gram_copy(c, o, p).start()
        if p < space - 1:
            gram_copy(core, m, jnp.where(p < z, p, p + 1)).start()
    own = pltpu.make_async_copy(g_send.at[core], g_recv.at[mine], g_got)
    own.start()
    trade(chunks - 1).start()

    def put(ref, q, start):
        place = pl.ds(pl.multiple_of(start * rows + q * width, width), width)
        for r in range(2):
            for f in range(half):
                first = r * n + f * nb
                x_out[first : first + nb, place] = ref[r, pl.ds(f, nb, stride=half), :]

    for q in range(chunks):
        put(spec.at[q, core], q, core)
    wait(inbox, p_recv)
    for q in range(chunks):
        put(inbox.at[q], q, other)
    wait(inbox, p_send)
    if exchange and space > 1:
        wait(recv.at[: space - 1], s_send)
    wait(g_recv, g_got)
    slots = [g_recv[s] for s in range(2 * space * tm)]
    while len(slots) > 1:
        slots = [
            sum(slots[i + 1 : i + 2], slots[i]) for i in range(0, len(slots), 2)
        ]
    g_out[...] = slots[0] * (1.0 / total)
    wait(g_recv.at[: g_recv.shape[0] - 1], g_sent)


def modes_kernel(half, gram, x, modes, upper):
    nb, lanes = gram.shape
    row = lax.broadcasted_iota(jnp.int32, (nb, lanes), 0)
    lane = lax.broadcasted_iota(jnp.int32, (nb, lanes), 1)
    col = lane % nb
    which = lane // nb

    def pick(a, index):
        return jnp.take_along_axis(a, index, axis=1, mode="promise_in_bounds")

    mixed = pick(gram[...], col * half + which)
    turned = mixed.T
    turned = jnp.concatenate(
        [turned[f * nb : (f + 1) * nb] for f in range(half)], axis=1
    )
    re = (mixed + turned) * 0.5 + jnp.where(row == col, epsilon, 0.0)
    im = (mixed - turned) * 0.5
    diag = jnp.zeros_like(re)
    for p in range(nb):
        index = which * nb + p
        cr, ci = pick(re, index), pick(im, index)
        diag = jnp.where(row == p, cr, diag)
        if p == nb - 1:
            break
        inv = 1.0 / cr[p : p + 1]
        mr, mi = cr * inv, ci * inv
        pr, pi = re[p : p + 1], im[p : p + 1]
        here = col == p
        nr = jnp.where(here, 0.0, re) - (
            mr * jnp.where(here[:1], 1.0, pr) - mi * jnp.where(here[:1], 0.0, pi)
        )
        ni = jnp.where(here, 0.0, im) - (
            mr * jnp.where(here[:1], 0.0, pi) + mi * jnp.where(here[:1], 1.0, pr)
        )
        re = jnp.where(row > p, nr, re)
        im = jnp.where(row > p, ni, im)
    pivot = jnp.sqrt(diag)
    scale = 1.0 / pivot
    re, im = re * scale, im * scale
    ur = jnp.where(col > row, re, jnp.where(col == row, pivot, 0.0))
    ui = jnp.where(col > row, im, 0.0)
    lr = jnp.where(col < row, re, jnp.where(col == row, scale, 0.0))
    li = jnp.where(col < row, im, 0.0)
    for f in range(half):
        upper[0, f] = ur[:, f * nb : (f + 1) * nb]
        upper[1, f] = ui[:, f * nb : (f + 1) * nb]
    parts = []
    for f in range(half):
        fr = jnp.where(which == f, lr, 0.0)
        fi = jnp.where(which == f, li, 0.0)
        parts.append(jnp.concatenate([fr, fi], axis=1))
        parts.append(jnp.concatenate([-fi, fr], axis=1))
    big = jnp.concatenate(parts, axis=0)
    out = jnp.dot(big, x[...], precision=HIGHEST, preferred_element_type=jnp.float32)
    modes[...] = out.reshape(modes.shape)


def in_hbm(a):
    return pltpu.with_memory_space_constraint(a, pltpu.HBM)


def on_device(snapshots, weights):
    freq = lax.axis_size("freq")
    space = lax.axis_size("space")
    tm = lax.axis_size("tm")
    assert freq == 2
    half = NF // freq
    nb, local_times, columns = snapshots.shape
    rows = columns // (space * freq)
    exchange = local_times % 8 == 0
    if not exchange:
        shaped = snapshots.reshape(nb, local_times, space, freq, rows)
        own = lax.dynamic_index_in_dim(shaped, lax.axis_index("freq"), 3, keepdims=False)
        pieces = lax.all_to_all(own, "space", split_axis=2, concat_axis=1, tiled=True)
        snapshots = pieces.reshape(nb, SEGMENT_FRAMES, rows)
    senders = space if exchange else 1
    times = SEGMENT_FRAMES // senders
    chunks = rows // min(rows, LANES)
    table = jnp.asarray(dft_table(half, senders, times))
    weight = weights.reshape(freq, 1, rows)
    lanes = nb * half
    peers = freq * space * tm
    vmem = pl.BlockSpec(memory_space=pltpu.VMEM)
    dma = pltpu.SemaphoreType.DMA
    x, gram = pl.pallas_call(
        functools.partial(
            spectra_kernel, exchange, space, tm, weights.shape[0] * space * tm
        ),
        out_shape=(
            pltpu.VMEM((2 * lanes, freq * rows), jnp.float32),
            pltpu.VMEM((nb, lanes), jnp.float32),
        ),
        in_specs=[pl.BlockSpec(memory_space=pltpu.HBM)] * 3,
        out_specs=(vmem, vmem),
        scratch_shapes=[
            pltpu.VMEM(weight.shape, jnp.float32),
            pltpu.VMEM(table.shape, jnp.float32),
            pltpu.VMEM((senders, nb, times, rows), jnp.float32),
            pltpu.VMEM((chunks, freq, 2, lanes, rows // chunks), jnp.float32),
            pltpu.VMEM((chunks, 2, lanes, rows // chunks), jnp.float32),
            pltpu.VMEM((freq, lanes, lanes), jnp.float32),
            pltpu.VMEM((freq, nb, lanes), jnp.float32),
            pltpu.VMEM((peers, nb, lanes), jnp.float32),
            dma((2,)),
            dma,
            dma((chunks,)),
            dma,
            dma,
            dma,
            dma,
            pltpu.SemaphoreType.REGULAR((space,)),
            pltpu.SemaphoreType.REGULAR,
        ],
        compiler_params=pltpu.CompilerParams(
            collective_id=0, has_side_effects=True, vmem_limit_bytes=52 * 2**20
        ),
        name="spectra",
    )(snapshots, in_hbm(weight), in_hbm(table))
    modes, upper = pl.pallas_call(
        functools.partial(modes_kernel, half),
        out_shape=(
            jax.ShapeDtypeStruct((half, 2, nb, freq * rows), jnp.float32),
            jax.ShapeDtypeStruct((2, half, nb, nb), jnp.float32),
        ),
        in_specs=[vmem, vmem],
        out_specs=(vmem, vmem),
        compiler_params=pltpu.CompilerParams(vmem_limit_bytes=40 * 2**20),
        name="modes",
    )(gram, x)
    return modes, upper


def solution(mesh):
    return jax.shard_map(
        on_device,
        mesh=mesh,
        in_specs=(P(None, "space", ("groups", "tm")), P(("groups", "tm", "space"))),
        out_specs=(
            P("freq", None, None, ("groups", "tm", "space")),
            P("groups", "freq", None, None),
        ),
        check_vma=False,
    )
```

```python
import functools

import jax
import jax.numpy as jnp
import numpy as np
from jax import lax
from jax.experimental import pallas as pl
from jax.experimental.pallas import tpu as pltpu
from jax.sharding import PartitionSpec as P

SEGMENT_FRAMES = 64
NF = 16
GROUP = 4
LANES = 128
PACK = 4
PANEL = 8

epsilon = 1e-05
MESH = pl.DeviceIdType.MESH
HIGHEST = lax.Precision.HIGHEST


def dft_table(half, senders, local_times):
    moments = np.arange(SEGMENT_FRAMES)
    hann = 0.5 - 0.5 * np.cos(2.0 * np.pi * moments / SEGMENT_FRAMES)
    taper = hann / np.sqrt(np.sum(hann * hann))
    angle = (np.arange(NF) + 1)[:, None] * moments[None, :] % SEGMENT_FRAMES
    phase = 2.0 * np.pi * angle / SEGMENT_FRAMES
    pair = np.stack([np.cos(phase) * taper, -np.sin(phase) * taper])
    pair = pair.reshape(2, NF // half, half, senders, local_times)
    full = np.einsum("rhfzt,bc->hrbfzct", pair, np.eye(GROUP))
    shape = (2 * NF * GROUP, senders * GROUP * local_times)
    return full.reshape(shape).astype(np.float32)


def send_order(k, space, chunks):
    middle = space // 2
    halves = [p for p in range(middle)], [p for p in range(middle, space)]
    here, there = halves if k < middle else halves[::-1]
    cross = sorted(there, key=lambda p: -abs(p - k))
    near = [p for p in here if p != k]
    early, late = cross[:-1], cross[-1:]
    order = [(0, p) for p in late]
    if k in (middle - 1, middle):
        order += [(q, p) for q in range(chunks) for p in early]
        order += [(q, p) for q in range(chunks) for p in near + late]
    else:
        order += [(q, p) for q in range(chunks) for p in early + near]
        order += [(q, p) for q in range(chunks) for p in late]
    return list(dict.fromkeys(order))


def split(a):
    first = a.astype(jnp.bfloat16)
    rest = a - first.astype(jnp.float32)
    middle = rest.astype(jnp.bfloat16)
    last = (rest - middle.astype(jnp.float32)).astype(jnp.bfloat16)
    return first, middle, last


def spectra_kernel(
    exchange, space, tm, total, snap, weight_in, table_in, x_out, low_out, g_out,
    weight, table, recv, spec, inbox, acc, g_send, g_recv,
    c_sem, s_send, s_recv, p_send, p_recv, g_sent, g_got, here, ready,
):
    core = lax.axis_index("freq")
    z = lax.axis_index("space")
    m = lax.axis_index("tm")
    other = 1 - core
    nb, rows = recv.shape[1], recv.shape[3]
    width = min(rows, LANES)
    chunks = rows // width
    half = NF // 2
    n = nb * half
    lines = [(c, lax.rem(m + d, tm)) for d in range(tm) for c in (core, other)][1:]

    mine = (core * tm + m) * space + z

    def cols(q):
        return pl.ds(q * width, width)

    def source(p, q):
        start = (p * 2 + core) * rows + q * width
        return snap.at[:, :, pl.ds(pl.multiple_of(start, width), width)]

    def local(q):
        return pltpu.make_async_copy(
            source(z, q) if exchange else snap.at[:, :, cols(q)],
            recv.at[z if exchange else 0, :, :, cols(q)],
            s_recv.at[q],
        )

    def send(q, p):
        return pltpu.make_async_remote_copy(
            src_ref=source(p, q),
            dst_ref=recv.at[z, :, :, cols(q)],
            send_sem=s_send,
            recv_sem=s_recv.at[q],
            device_id={"space": p},
            device_id_type=MESH,
        )

    def wait(ref, semaphore):
        pltpu.make_async_copy(ref, ref, semaphore).wait()

    def trade(q):
        return pltpu.make_async_remote_copy(
            src_ref=spec.at[q, other],
            dst_ref=inbox.at[q],
            send_sem=p_send,
            recv_sem=p_recv,
            device_id={"freq": other},
            device_id_type=MESH,
        )

    def gram_copy(c, o, p):
        return pltpu.make_async_remote_copy(
            src_ref=g_send.at[c],
            dst_ref=g_recv.at[mine],
            send_sem=g_sent,
            recv_sem=g_got,
            device_id={"freq": c, "tm": o, "space": p},
            device_id_type=MESH,
        )

    def greet(semaphore, **place):
        pl.semaphore_signal(
            semaphore, inc=1, device_id=place, device_id_type=MESH
        )

    barrier = pltpu.get_barrier_semaphore()
    for p in range(1, space):
        @pl.when(z < p)
        def _():
            greet(barrier, space=p)

    @pl.when(z > 0)
    def _():
        pl.semaphore_wait(barrier, z)

    for p in range(space - 1):
        @pl.when(z > p)
        def _():
            greet(here.at[z], space=p)

    for k in range(space):
        @pl.when(z == k)
        def _():
            met = set(range(k + 1))
            for q, p in send_order(k, space, chunks) if exchange else ():
                if p not in met:
                    pl.semaphore_wait(here.at[p], 1)
                    met.add(p)
                send(q, p).start()
            for p in range(space):
                if p not in met:
                    pl.semaphore_wait(here.at[p], 1)

    constants = [
        pltpu.make_async_copy(weight_in, weight, c_sem.at[0]),
        pltpu.make_async_copy(table_in, table, c_sem.at[1]),
    ]
    for copy in constants:
        copy.start()
    for q in range(chunks):
        local(q).start()

    @pl.when(z == 0)
    def _():
        for c, o in lines:
            greet(barrier, freq=c, tm=o)
        pl.semaphore_wait(barrier, len(lines))
        for p in range(1, space):
            greet(ready, space=p)

    @pl.when(z > 0)
    def _():
        pl.semaphore_wait(ready, 1)

    for copy in constants:
        copy.wait()

    for q in range(chunks):
        wait(recv.at[:, :, :, cols(q)], s_recv.at[q])
        flat = [
            recv[:, b : b + GROUP, :, q * width : (q + 1) * width].reshape(-1, width)
            for b in range(0, nb, GROUP)
        ]
        got = jnp.dot(
            table[...], jnp.concatenate(flat, axis=1),
            precision=HIGHEST, preferred_element_type=jnp.float32,
        )
        step = GROUP * half
        w = weight[core, :, q * width : (q + 1) * width]
        for c in range(2):
            pair = []
            for r in range(2):
                top = (c * 2 + r) * step
                pair.append(
                    jnp.concatenate(
                        [
                            got[top : top + step, g * width : (g + 1) * width]
                            for g in range(nb // GROUP)
                        ],
                        axis=0,
                    )
                )
                spec[q, c, r] = pair[r]
            re, im = pair
            left = jnp.concatenate([re * w, im * w], axis=1)
            right = jnp.concatenate([re + im, im - re], axis=1)
            product = lax.dot_general(
                left, right, (((1,), (1,)), ((), ())),
                precision=HIGHEST, preferred_element_type=jnp.float32,
            )
            acc[c] = product if q == 0 else acc[c] + product
        if q < chunks - 1:
            trade(q).start()

    lane = lax.broadcasted_iota(jnp.int32, (nb, n), 1)
    for c in range(2):
        out = acc[c, pl.ds(0, nb, stride=half), :]
        for f in range(1, half):
            out = jnp.where(
                lane % half == f, acc[c, pl.ds(f, nb, stride=half), :], out
            )
        g_send[c] = out
    for p in range(space):
        for c, o in lines:
            gram_copy(c, o, p).start()
        if p < space - 1:
            gram_copy(core, m, jnp.where(p < z, p, p + 1)).start()
    own = pltpu.make_async_copy(g_send.at[core], g_recv.at[mine], g_got)
    own.start()
    trade(chunks - 1).start()

    def put(ref, q, start):
        place = pl.ds(pl.multiple_of(start * rows + q * width, width), width)
        for r in range(2):
            for f in range(half):
                first, middle, last = split(ref[r, pl.ds(f, nb, stride=half), :])
                g, top = f // PACK, (r * PACK + f % PACK) * nb
                x_out[g, 0, top : top + nb, place] = first
                x_out[g, 1, top : top + nb, place] = middle
                low_out[g, top : top + nb, place] = last

    for q in range(chunks):
        put(spec.at[q, core], q, core)
    wait(inbox, p_recv)
    for q in range(chunks):
        put(inbox.at[q], q, other)
    wait(inbox, p_send)
    if exchange and space > 1:
        wait(recv.at[: space - 1], s_send)
    wait(g_recv, g_got)
    slots = [g_recv[s] for s in range(2 * space * tm)]
    while len(slots) > 1:
        slots = [
            sum(slots[i + 1 : i + 2], slots[i]) for i in range(0, len(slots), 2)
        ]
    g_out[...] = slots[0] * (1.0 / total)
    wait(g_recv.at[: g_recv.shape[0] - 1], g_sent)


def modes_kernel(half, gram, x, low, modes, upper, out, triangle, m_sem, u_sem):
    nb, lanes = gram.shape
    row = lax.broadcasted_iota(jnp.int32, (nb, lanes), 0)
    lane = lax.broadcasted_iota(jnp.int32, (nb, lanes), 1)
    col = lane % nb
    which = lane // nb

    def pick(a, index):
        return jnp.take_along_axis(a, index, axis=1, mode="promise_in_bounds")

    mixed = pick(gram[...], col * half + which)
    turned = mixed.T
    turned = jnp.concatenate(
        [turned[f * nb : (f + 1) * nb] for f in range(half)], axis=1
    )
    re = (mixed + turned) * 0.5 + jnp.where(row == col, epsilon, 0.0)
    im = (mixed - turned) * 0.5
    diag = jnp.zeros_like(re)
    for start in range(0, nb, PANEL):
        panel = []
        for p in range(start, start + PANEL):
            index = which * nb + p
            panel.append((pick(re, index), pick(im, index)))
        for p in range(start, start + PANEL):
            cr, ci = panel[p - start]
            diag = jnp.where(row == p, cr, diag)
            if p == nb - 1:
                break
            inv = 1.0 / cr[p : p + 1]
            mr, mi = cr * inv, ci * inv
            for k in range(p - start + 1, PANEL):
                kr, ki = panel[k]
                sr, si = kr[p : p + 1], ki[p : p + 1]
                panel[k] = kr - (mr * sr - mi * si), ki - (mr * si + mi * sr)
            pr, pi = re[p : p + 1], im[p : p + 1]
            here = col == p
            nr = jnp.where(here, 0.0, re) - (
                mr * jnp.where(here[:1], 1.0, pr) - mi * jnp.where(here[:1], 0.0, pi)
            )
            ni = jnp.where(here, 0.0, im) - (
                mr * jnp.where(here[:1], 0.0, pi) + mi * jnp.where(here[:1], 1.0, pr)
            )
            re = jnp.where(row > p, nr, re)
            im = jnp.where(row > p, ni, im)
    pivot = jnp.sqrt(diag)
    scale = 1.0 / pivot
    re, im = re * scale, im * scale
    lr = jnp.where(col < row, re, jnp.where(col == row, scale, 0.0))
    li = jnp.where(col < row, im, 0.0)
    left = lane < PACK * nb
    other_r = pltpu.roll(lr, PACK * nb, axis=1)
    other_i = pltpu.roll(li, PACK * nb, axis=1)
    tops = (
        (jnp.where(left, lr, other_i), jnp.where(left, -li, other_r)),
        (jnp.where(left, other_r, li), jnp.where(left, -other_i, lr)),
    )
    spot = which % PACK
    copies = []
    span = x.shape[-1] // 2
    for g in range(half // PACK):
        parts = [[], [], []]
        for k in range(PACK):
            for block in tops[g]:
                for level, term in zip(parts, split(jnp.where(spot == k, block, 0.0))):
                    level.append(term)
        first, middle, last = (jnp.concatenate(level, axis=0) for level in parts)
        stack = jnp.concatenate(
            [
                jnp.concatenate([first, first], axis=1),
                jnp.concatenate([middle, middle], axis=1),
                jnp.concatenate([last, jnp.zeros_like(last)], axis=1),
            ],
            axis=0,
        )
        n = first.shape[0]
        for c in range(2):
            place = pl.ds(c * span, span)
            high = x[g, :, :, place].reshape(2 * n, span)
            got = jnp.dot(stack, high, preferred_element_type=jnp.float32)
            small = jnp.dot(first, low[g, :, place], preferred_element_type=jnp.float32)
            total = got[:n] + (got[n : 2 * n] + (got[2 * n :] + small))
            out[g, :, :, :, place] = total.reshape(PACK, 2, nb, span)
            copies.append(
                pltpu.make_async_copy(
                    out.at[g, :, :, :, place],
                    modes.at[pl.ds(g * PACK, PACK), :, :, place],
                    m_sem.at[g, c],
                )
            )
            copies[-1].start()
        if g == 0:
            ur = jnp.where(col > row, re, jnp.where(col == row, pivot, 0.0))
            ui = jnp.where(col > row, im, 0.0)
            for f in range(half):
                triangle[0, f] = ur[:, f * nb : (f + 1) * nb]
                triangle[1, f] = ui[:, f * nb : (f + 1) * nb]
            copies.append(pltpu.make_async_copy(triangle, upper, u_sem))
            copies[-1].start()
    for copy in copies:
        copy.wait()


def modes_call(gram, x, low):
    nb, lanes = gram.shape
    half = lanes // nb
    columns = x.shape[-1]
    vmem = pl.BlockSpec(memory_space=pltpu.VMEM)
    hbm = pl.BlockSpec(memory_space=pltpu.HBM)
    dma = pltpu.SemaphoreType.DMA
    groups = half // PACK
    return pl.pallas_call(
        functools.partial(modes_kernel, half),
        out_shape=(
            jax.ShapeDtypeStruct((half, 2, nb, columns), jnp.float32),
            jax.ShapeDtypeStruct((2, half, nb, nb), jnp.float32),
        ),
        in_specs=[vmem, vmem, vmem],
        out_specs=(hbm, hbm),
        scratch_shapes=[
            pltpu.VMEM((groups, PACK, 2, nb, columns), jnp.float32),
            pltpu.VMEM((2, half, nb, nb), jnp.float32),
            dma((groups, 2)),
            dma,
        ],
        compiler_params=pltpu.CompilerParams(vmem_limit_bytes=40 * 2**20),
        name="modes",
    )(gram, x, low)


def in_hbm(a):
    return pltpu.with_memory_space_constraint(a, pltpu.HBM)


def on_device(snapshots, weights):
    freq = lax.axis_size("freq")
    space = lax.axis_size("space")
    tm = lax.axis_size("tm")
    assert freq == 2
    half = NF // freq
    nb, local_times, columns = snapshots.shape
    rows = columns // (space * freq)
    exchange = local_times % 8 == 0
    if not exchange:
        shaped = snapshots.reshape(nb, local_times, space, freq, rows)
        own = lax.dynamic_index_in_dim(shaped, lax.axis_index("freq"), 3, keepdims=False)
        pieces = lax.all_to_all(own, "space", split_axis=2, concat_axis=1, tiled=True)
        snapshots = pieces.reshape(nb, SEGMENT_FRAMES, rows)
    senders = space if exchange else 1
    times = SEGMENT_FRAMES // senders
    chunks = rows // min(rows, LANES)
    table = jnp.asarray(dft_table(half, senders, times))
    weight = weights.reshape(freq, 1, rows)
    lanes = nb * half
    peers = freq * space * tm
    vmem = pl.BlockSpec(memory_space=pltpu.VMEM)
    dma = pltpu.SemaphoreType.DMA
    x, low, gram = pl.pallas_call(
        functools.partial(
            spectra_kernel, exchange, space, tm, weights.shape[0] * space * tm
        ),
        out_shape=(
            pltpu.VMEM((half // PACK, 2, 2 * PACK * nb, freq * rows), jnp.bfloat16),
            pltpu.VMEM((half // PACK, 2 * PACK * nb, freq * rows), jnp.bfloat16),
            pltpu.VMEM((nb, lanes), jnp.float32),
        ),
        in_specs=[pl.BlockSpec(memory_space=pltpu.HBM)] * 3,
        out_specs=(vmem, vmem, vmem),
        scratch_shapes=[
            pltpu.VMEM(weight.shape, jnp.float32),
            pltpu.VMEM(table.shape, jnp.float32),
            pltpu.VMEM((senders, nb, times, rows), jnp.float32),
            pltpu.VMEM((chunks, freq, 2, lanes, rows // chunks), jnp.float32),
            pltpu.VMEM((chunks, 2, lanes, rows // chunks), jnp.float32),
            pltpu.VMEM((freq, lanes, lanes), jnp.float32),
            pltpu.VMEM((freq, nb, lanes), jnp.float32),
            pltpu.VMEM((peers, nb, lanes), jnp.float32),
            dma((2,)),
            dma,
            dma((chunks,)),
            dma,
            dma,
            dma,
            dma,
            pltpu.SemaphoreType.REGULAR((space,)),
            pltpu.SemaphoreType.REGULAR,
        ],
        compiler_params=pltpu.CompilerParams(
            collective_id=0, has_side_effects=True, vmem_limit_bytes=52 * 2**20
        ),
        name="spectra",
    )(snapshots, in_hbm(weight), in_hbm(table))
    modes, upper = modes_call(gram, x, low)
    return modes, upper


def solution(mesh):
    return jax.shard_map(
        on_device,
        mesh=mesh,
        in_specs=(P(None, "space", ("groups", "tm")), P(("groups", "tm", "space"))),
        out_specs=(
            P("freq", None, None, ("groups", "tm", "space")),
            P("groups", "freq", None, None),
        ),
        check_vma=False,
    )
```

```python
import functools

import jax
import jax.numpy as jnp
import numpy as np
from jax import lax
from jax.experimental import pallas as pl
from jax.experimental.pallas import tpu as pltpu
from jax.sharding import PartitionSpec as P

SEGMENT_FRAMES = 64
NF = 16
GROUP = 4
LANES = 128
PACK = 4
PANEL = 8

epsilon = 1e-05
MESH = pl.DeviceIdType.MESH
HIGHEST = lax.Precision.HIGHEST


def dft_table(half, senders, local_times):
    moments = np.arange(SEGMENT_FRAMES)
    hann = 0.5 - 0.5 * np.cos(2.0 * np.pi * moments / SEGMENT_FRAMES)
    taper = hann / np.sqrt(np.sum(hann * hann))
    angle = (np.arange(NF) + 1)[:, None] * moments[None, :] % SEGMENT_FRAMES
    phase = 2.0 * np.pi * angle / SEGMENT_FRAMES
    pair = np.stack([np.cos(phase) * taper, -np.sin(phase) * taper])
    pair = pair.reshape(2, NF // half, half, senders, local_times)
    full = np.einsum("rhfzt,bc->hrbfzct", pair, np.eye(GROUP))
    shape = (2 * NF * GROUP, senders * GROUP * local_times)
    return full.reshape(shape).astype(np.float32)


def send_order(k, space, chunks):
    middle = space // 2
    halves = [p for p in range(middle)], [p for p in range(middle, space)]
    here, there = halves if k < middle else halves[::-1]
    cross = sorted(there, key=lambda p: -abs(p - k))
    near = [p for p in here if p != k]
    early, late = cross[:-1], cross[-1:]
    order = [(q, p) for p in late for q in range(2)]
    if k in (middle - 1, middle):
        order += [(q, p) for q in range(chunks) for p in early]
        order += [(q, p) for q in range(chunks) for p in near + late]
    else:
        order += [(q, p) for q in range(chunks) for p in early + near]
        order += [(q, p) for q in range(chunks) for p in late]
    return list(dict.fromkeys(order))


def split(a):
    first = a.astype(jnp.bfloat16)
    rest = a - first.astype(jnp.float32)
    middle = rest.astype(jnp.bfloat16)
    last = (rest - middle.astype(jnp.float32)).astype(jnp.bfloat16)
    return first, middle, last


def spectra_kernel(
    exchange, space, tm, total, snap, weight_in, table_in, x_out, low_out, g_out,
    weight, table, recv, spec, inbox, acc, g_side, g_send, g_recv,
    c_sem, s_send, s_recv, p_send, p_recv, g_sent, g_got, f_sent, f_got, here, ready,
):
    core = lax.axis_index("freq")
    z = lax.axis_index("space")
    m = lax.axis_index("tm")
    other = 1 - core
    chunks, nb, width = recv.shape[0], recv.shape[2], recv.shape[4]
    rows = chunks * width
    half = NF // 2
    n = nb * half
    lines = [(core, lax.rem(m + d, tm)) for d in range(1, tm)]
    mine = m * space + z

    def cols(q):
        return pl.ds(q * width, width)

    def source(p, q):
        start = (p * 2 + core) * rows + q * width
        return snap.at[:, :, pl.ds(pl.multiple_of(start, width), width)]

    def local(q):
        return pltpu.make_async_copy(
            source(z, q) if exchange else snap.at[:, :, cols(q)],
            recv.at[q, z if exchange else 0],
            s_recv.at[q],
        )

    def send(q, p):
        return pltpu.make_async_remote_copy(
            src_ref=source(p, q),
            dst_ref=recv.at[q, z],
            send_sem=s_send,
            recv_sem=s_recv.at[q],
            device_id={"space": p},
            device_id_type=MESH,
        )

    def wait(ref, semaphore):
        pltpu.make_async_copy(ref, ref, semaphore).wait()

    def trade(q):
        return pltpu.make_async_remote_copy(
            src_ref=spec.at[q, other],
            dst_ref=inbox.at[q],
            send_sem=p_send,
            recv_sem=p_recv,
            device_id={"freq": other},
            device_id_type=MESH,
        )

    def gram_copy(o, p):
        return pltpu.make_async_remote_copy(
            src_ref=g_send,
            dst_ref=g_recv.at[mine],
            send_sem=g_sent,
            recv_sem=g_got,
            device_id={"tm": o, "space": p},
            device_id_type=MESH,
        )

    def fold():
        return pltpu.make_async_remote_copy(
            src_ref=g_side.at[0],
            dst_ref=g_side.at[1],
            send_sem=f_sent,
            recv_sem=f_got,
            device_id={"freq": other},
            device_id_type=MESH,
        )

    lane = lax.broadcasted_iota(jnp.int32, (nb, n), 1)

    def diagonal(c):
        out = acc[c, pl.ds(0, nb, stride=half), :]
        for f in range(1, half):
            out = jnp.where(
                lane % half == f, acc[c, pl.ds(f, nb, stride=half), :], out
            )
        return out

    def greet(semaphore, **place):
        pl.semaphore_signal(
            semaphore, inc=1, device_id=place, device_id_type=MESH
        )

    barrier = pltpu.get_barrier_semaphore()
    head, pair = space - 1, (space // 2 - 1, space // 2)
    inner = pair if exchange and space > 3 else ()

    @pl.when(z < head)
    def _():
        greet(barrier, space=head)

    for k in reversed(range(space)):
        @pl.when(z == k)
        def _():
            order = send_order(k, space, chunks) if exchange else []
            if k in inner:
                mate = sum(inner) - k
                greet(barrier, space=mate)
                pl.semaphore_wait(barrier, 1)
                while order[0][1] == mate:
                    send(*order.pop(0)).start()
            if k < head:
                pl.semaphore_wait(here, 1)
            elif k > 0:
                pl.semaphore_wait(barrier, head)
                for p in reversed(range(head)):
                    greet(here, space=p)
            for q, p in order:
                send(q, p).start()

    constants = [
        pltpu.make_async_copy(weight_in, weight, c_sem.at[0]),
        pltpu.make_async_copy(table_in, table, c_sem.at[1]),
    ]
    for copy in constants:
        copy.start()
    for q in range(chunks):
        local(q).start()

    @pl.when(z == 0)
    def _():
        for c, o in [*lines, (other, m)]:
            greet(barrier, freq=c, tm=o)
        pl.semaphore_wait(barrier, len(lines) + 1)
        for p in range(1, space):
            greet(ready, space=p)

    @pl.when(z > 0)
    def _():
        pl.semaphore_wait(ready, 1)

    for copy in constants:
        copy.wait()

    acc[...] = jnp.zeros_like(acc)
    step = GROUP * half

    @pl.loop(0, chunks)
    def _(q):
        wait(recv.at[q], s_recv.at[q])
        flat = [
            recv[q, :, b : b + GROUP].reshape(-1, width) for b in range(0, nb, GROUP)
        ]
        got = jnp.dot(
            table[...], jnp.concatenate(flat, axis=1),
            precision=HIGHEST, preferred_element_type=jnp.float32,
        )
        for c in range(2):
            for r in range(2):
                top = (c * 2 + r) * step
                for g in range(nb // GROUP):
                    spec[q, c, r, g * step : (g + 1) * step] = got[
                        top : top + step, g * width : (g + 1) * width
                    ]
        w = weight[core, q]
        for c in (other, core):
            re, im = spec[q, c, 0], spec[q, c, 1]
            left = jnp.concatenate([re * w, im * w], axis=1)
            right = jnp.concatenate([re + im, im - re], axis=1)
            acc[c] += lax.dot_general(
                left, right, (((1,), (1,)), ((), ())),
                precision=HIGHEST, preferred_element_type=jnp.float32,
            )
            if c is other:
                @pl.when(q == chunks - 1)
                def _():
                    g_side[0] = diagonal(other)
                    fold().start()

        trade(q).start()

    part = diagonal(core)
    fold().wait_recv()
    g_send[...] = part + g_side[1]
    for p in range(space):
        for _, o in lines:
            gram_copy(o, p).start()
        if p < space - 1:
            gram_copy(m, jnp.where(p < z, p, p + 1)).start()
    own = pltpu.make_async_copy(g_send, g_recv.at[mine], g_got)
    own.start()

    def put(ref, q, start):
        place = pl.ds(pl.multiple_of(start * rows + q * width, width), width)
        for r in range(2):
            for f in range(half):
                first, middle, last = split(ref[r, pl.ds(f, nb, stride=half), :])
                g, top = f // PACK, (r * PACK + f % PACK) * nb
                x_out[g, 0, top : top + nb, place] = first
                x_out[g, 1, top : top + nb, place] = middle
                low_out[g, top : top + nb, place] = last

    @pl.loop(0, chunks)
    def _(q):
        put(spec.at[q, core], q, core)

    wait(inbox, p_recv)

    @pl.loop(0, chunks)
    def _(q):
        put(inbox.at[q], q, other)

    wait(inbox, p_send)
    if exchange and space > 1:
        wait(recv.at[:, : space - 1], s_send)
    wait(g_recv, g_got)
    slots = [g_recv[s] for s in range(space * tm)]
    while len(slots) > 1:
        slots = [
            sum(slots[i + 1 : i + 2], slots[i]) for i in range(0, len(slots), 2)
        ]
    g_out[...] = slots[0] * (1.0 / total)
    fold().wait_send()
    if space * tm > 1:
        wait(g_recv.at[: space * tm - 1], g_sent)


def modes_kernel(half, gram, x, low, modes, upper, out, triangle, m_sem, u_sem):
    nb, lanes = gram.shape
    row = lax.broadcasted_iota(jnp.int32, (nb, lanes), 0)
    lane = lax.broadcasted_iota(jnp.int32, (nb, lanes), 1)
    col = lane % nb
    which = lane // nb

    def pick(a, index):
        return jnp.take_along_axis(a, index, axis=1, mode="promise_in_bounds")

    mixed = pick(gram[...], col * half + which)
    turned = mixed.T
    turned = jnp.concatenate(
        [turned[f * nb : (f + 1) * nb] for f in range(half)], axis=1
    )
    re = (mixed + turned) * 0.5 + jnp.where(row == col, epsilon, 0.0)
    im = (mixed - turned) * 0.5
    diag = jnp.zeros_like(re)
    for start in range(0, nb, PANEL):
        panel = []
        for p in range(start, start + PANEL):
            index = which * nb + p
            panel.append((pick(re, index), pick(im, index)))
        for p in range(start, start + PANEL):
            cr, ci = panel[p - start]
            diag = jnp.where(row == p, cr, diag)
            if p == nb - 1:
                break
            inv = 1.0 / cr[p : p + 1]
            mr, mi = cr * inv, ci * inv
            for k in range(p - start + 1, PANEL):
                kr, ki = panel[k]
                sr, si = kr[p : p + 1], ki[p : p + 1]
                panel[k] = kr - (mr * sr - mi * si), ki - (mr * si + mi * sr)
            pr, pi = re[p : p + 1], im[p : p + 1]
            here = col == p
            nr = jnp.where(here, 0.0, re) - (
                mr * jnp.where(here[:1], 1.0, pr) - mi * jnp.where(here[:1], 0.0, pi)
            )
            ni = jnp.where(here, 0.0, im) - (
                mr * jnp.where(here[:1], 0.0, pi) + mi * jnp.where(here[:1], 1.0, pr)
            )
            re = jnp.where(row > p, nr, re)
            im = jnp.where(row > p, ni, im)
    pivot = jnp.sqrt(diag)
    scale = 1.0 / pivot
    re, im = re * scale, im * scale
    lr = jnp.where(col < row, re, jnp.where(col == row, scale, 0.0))
    li = jnp.where(col < row, im, 0.0)
    left = lane < PACK * nb
    other_r = pltpu.roll(lr, PACK * nb, axis=1)
    other_i = pltpu.roll(li, PACK * nb, axis=1)
    tops = (
        (jnp.where(left, lr, other_i), jnp.where(left, -li, other_r)),
        (jnp.where(left, other_r, li), jnp.where(left, -other_i, lr)),
    )
    spot = which % PACK
    copies = []
    span = x.shape[-1] // 2
    for g in range(half // PACK):
        parts = [[], [], []]
        for k in range(PACK):
            for block in tops[g]:
                for level, term in zip(parts, split(jnp.where(spot == k, block, 0.0))):
                    level.append(term)
        first, middle, last = (jnp.concatenate(level, axis=0) for level in parts)
        stack = jnp.concatenate(
            [
                jnp.concatenate([first, first], axis=1),
                jnp.concatenate([middle, middle], axis=1),
                jnp.concatenate([last, jnp.zeros_like(last)], axis=1),
            ],
            axis=0,
        )
        n = first.shape[0]
        for c in range(2):
            place = pl.ds(c * span, span)
            high = x[g, :, :, place].reshape(2 * n, span)
            got = jnp.dot(stack, high, preferred_element_type=jnp.float32)
            small = jnp.dot(first, low[g, :, place], preferred_element_type=jnp.float32)
            total = got[:n] + (got[n : 2 * n] + (got[2 * n :] + small))
            out[g, :, :, :, place] = total.reshape(PACK, 2, nb, span)
            copies.append(
                pltpu.make_async_copy(
                    out.at[g, :, :, :, place],
                    modes.at[pl.ds(g * PACK, PACK), :, :, place],
                    m_sem.at[g, c],
                )
            )
            copies[-1].start()
        if g == 0:
            ur = jnp.where(col > row, re, jnp.where(col == row, pivot, 0.0))
            ui = jnp.where(col > row, im, 0.0)
            for f in range(half):
                triangle[0, f] = ur[:, f * nb : (f + 1) * nb]
                triangle[1, f] = ui[:, f * nb : (f + 1) * nb]
            copies.append(pltpu.make_async_copy(triangle, upper, u_sem))
            copies[-1].start()
    for copy in copies:
        copy.wait()


def modes_call(gram, x, low):
    nb, lanes = gram.shape
    half = lanes // nb
    columns = x.shape[-1]
    vmem = pl.BlockSpec(memory_space=pltpu.VMEM)
    hbm = pl.BlockSpec(memory_space=pltpu.HBM)
    dma = pltpu.SemaphoreType.DMA
    groups = half // PACK
    return pl.pallas_call(
        functools.partial(modes_kernel, half),
        out_shape=(
            jax.ShapeDtypeStruct((half, 2, nb, columns), jnp.float32),
            jax.ShapeDtypeStruct((2, half, nb, nb), jnp.float32),
        ),
        in_specs=[vmem, vmem, vmem],
        out_specs=(hbm, hbm),
        scratch_shapes=[
            pltpu.VMEM((groups, PACK, 2, nb, columns), jnp.float32),
            pltpu.VMEM((2, half, nb, nb), jnp.float32),
            dma((groups, 2)),
            dma,
        ],
        compiler_params=pltpu.CompilerParams(vmem_limit_bytes=40 * 2**20),
        name="modes",
    )(gram, x, low)


def in_hbm(a):
    return pltpu.with_memory_space_constraint(a, pltpu.HBM)


def on_device(snapshots, weights):
    freq = lax.axis_size("freq")
    space = lax.axis_size("space")
    tm = lax.axis_size("tm")
    assert freq == 2
    half = NF // freq
    nb, local_times, columns = snapshots.shape
    rows = columns // (space * freq)
    exchange = local_times % 8 == 0
    if not exchange:
        shaped = snapshots.reshape(nb, local_times, space, freq, rows)
        own = lax.dynamic_index_in_dim(shaped, lax.axis_index("freq"), 3, keepdims=False)
        pieces = lax.all_to_all(own, "space", split_axis=2, concat_axis=1, tiled=True)
        snapshots = pieces.reshape(nb, SEGMENT_FRAMES, rows)
    senders = space if exchange else 1
    times = SEGMENT_FRAMES // senders
    chunks = rows // min(rows, LANES)
    weight = weights.reshape(freq, chunks, 1, rows // chunks)
    table = jnp.asarray(dft_table(half, senders, times))
    lanes = nb * half
    vmem = pl.BlockSpec(memory_space=pltpu.VMEM)
    dma = pltpu.SemaphoreType.DMA
    x, low, gram = pl.pallas_call(
        functools.partial(
            spectra_kernel, exchange, space, tm, weights.shape[0] * space * tm
        ),
        out_shape=(
            pltpu.VMEM((half // PACK, 2, 2 * PACK * nb, freq * rows), jnp.bfloat16),
            pltpu.VMEM((half // PACK, 2 * PACK * nb, freq * rows), jnp.bfloat16),
            pltpu.VMEM((nb, lanes), jnp.float32),
        ),
        in_specs=[pl.BlockSpec(memory_space=pltpu.HBM)] * 3,
        out_specs=(vmem, vmem, vmem),
        scratch_shapes=[
            pltpu.VMEM(weight.shape, jnp.float32),
            pltpu.VMEM(table.shape, jnp.float32),
            pltpu.VMEM((chunks, senders, nb, times, rows // chunks), jnp.float32),
            pltpu.VMEM((chunks, freq, 2, lanes, rows // chunks), jnp.float32),
            pltpu.VMEM((chunks, 2, lanes, rows // chunks), jnp.float32),
            pltpu.VMEM((freq, lanes, lanes), jnp.float32),
            pltpu.VMEM((2, nb, lanes), jnp.float32),
            pltpu.VMEM((nb, lanes), jnp.float32),
            pltpu.VMEM((space * tm, nb, lanes), jnp.float32),
            dma((2,)),
            dma,
            dma((chunks,)),
            dma,
            dma,
            dma,
            dma,
            dma,
            dma,
            pltpu.SemaphoreType.REGULAR,
            pltpu.SemaphoreType.REGULAR,
        ],
        compiler_params=pltpu.CompilerParams(
            collective_id=0, has_side_effects=True, vmem_limit_bytes=52 * 2**20
        ),
        name="spectra",
    )(snapshots, in_hbm(weight), in_hbm(table))
    modes, upper = modes_call(gram, x, low)
    return modes, upper


def solution(mesh):
    return jax.shard_map(
        on_device,
        mesh=mesh,
        in_specs=(P(None, "space", ("groups", "tm")), P(("groups", "tm", "space"))),
        out_specs=(
            P("freq", None, None, ("groups", "tm", "space")),
            P("groups", "freq", None, None),
        ),
        check_vma=False,
    )
```

```python
import functools

import jax
import jax.numpy as jnp
import numpy as np
from jax import lax
from jax.experimental import pallas as pl
from jax.experimental.pallas import tpu as pltpu
from jax.sharding import PartitionSpec as P

SEGMENT_FRAMES = 64
NF = 16
GROUP = 4
LANES = 128
PACK = 4
PANEL = 8

epsilon = 1e-05
MESH = pl.DeviceIdType.MESH
HIGHEST = lax.Precision.HIGHEST


def dft_table(half, senders, local_times):
    moments = np.arange(SEGMENT_FRAMES)
    hann = 0.5 - 0.5 * np.cos(2.0 * np.pi * moments / SEGMENT_FRAMES)
    taper = hann / np.sqrt(np.sum(hann * hann))
    angle = (np.arange(NF) + 1)[:, None] * moments[None, :] % SEGMENT_FRAMES
    phase = 2.0 * np.pi * angle / SEGMENT_FRAMES
    pair = np.stack([np.cos(phase) * taper, -np.sin(phase) * taper])
    pair = pair.reshape(2, NF // half, half, senders, local_times)
    full = np.einsum("rhfzt,bc->hrbfzct", pair, np.eye(GROUP))
    shape = (2 * NF * GROUP, senders * GROUP * local_times)
    return full.reshape(shape).astype(np.float32)


def send_order(k, space, chunks):
    middle = space // 2
    halves = [p for p in range(middle)], [p for p in range(middle, space)]
    here, there = halves if k < middle else halves[::-1]
    cross = sorted(there, key=lambda p: -abs(p - k))
    near = [p for p in here if p != k]
    early, late = cross[:-1], cross[-1:]
    order = [(q, p) for p in late for q in range(2)]
    if k in (middle - 1, middle):
        order += [(q, p) for q in range(chunks) for p in early]
        order += [(q, p) for q in range(chunks) for p in near + late]
    else:
        order += [(q, p) for q in range(chunks) for p in early + near]
        order += [(q, p) for q in range(chunks) for p in late]
    return list(dict.fromkeys(order))


def split(a):
    first = a.astype(jnp.bfloat16)
    rest = a - first.astype(jnp.float32)
    middle = rest.astype(jnp.bfloat16)
    last = (rest - middle.astype(jnp.float32)).astype(jnp.bfloat16)
    return first, middle, last


def spectra_kernel(
    exchange, space, tm, total, snap, weight_in, table_in, x_out, low_out, g_out,
    weight, table, recv, spec, inbox, acc, g_side, g_send, g_recv,
    c_sem, s_send, s_recv, p_send, p_recv, g_sent, g_got, f_sent, f_got, here, ready,
):
    core = lax.axis_index("freq")
    z = lax.axis_index("space")
    m = lax.axis_index("tm")
    other = 1 - core
    chunks, nb, width = recv.shape[0], recv.shape[2], recv.shape[4]
    rows = chunks * width
    half = NF // 2
    n = nb * half
    lines = [(core, lax.rem(m + d, tm)) for d in range(1, tm)]
    mine = m * space + z

    def cols(q):
        return pl.ds(q * width, width)

    def source(p, q):
        start = (p * 2 + core) * rows + q * width
        return snap.at[:, :, pl.ds(pl.multiple_of(start, width), width)]

    def local(q):
        return pltpu.make_async_copy(
            source(z, q) if exchange else snap.at[:, :, cols(q)],
            recv.at[q, z if exchange else 0],
            s_recv.at[q],
        )

    def send(q, p):
        return pltpu.make_async_remote_copy(
            src_ref=source(p, q),
            dst_ref=recv.at[q, z],
            send_sem=s_send,
            recv_sem=s_recv.at[q],
            device_id={"space": p},
            device_id_type=MESH,
        )

    def wait(ref, semaphore):
        pltpu.make_async_copy(ref, ref, semaphore).wait()

    def trade(q):
        return pltpu.make_async_remote_copy(
            src_ref=spec.at[q, other],
            dst_ref=inbox.at[q],
            send_sem=p_send,
            recv_sem=p_recv,
            device_id={"freq": other},
            device_id_type=MESH,
        )

    def gram_copy(o, p):
        return pltpu.make_async_remote_copy(
            src_ref=g_send,
            dst_ref=g_recv.at[mine],
            send_sem=g_sent,
            recv_sem=g_got,
            device_id={"tm": o, "space": p},
            device_id_type=MESH,
        )

    def fold():
        return pltpu.make_async_remote_copy(
            src_ref=g_side.at[0],
            dst_ref=g_side.at[1],
            send_sem=f_sent,
            recv_sem=f_got,
            device_id={"freq": other},
            device_id_type=MESH,
        )

    lane = lax.broadcasted_iota(jnp.int32, (nb, n), 1)

    def diagonal(c):
        out = acc[c, pl.ds(0, nb, stride=half), :]
        for f in range(1, half):
            out = jnp.where(
                lane % half == f, acc[c, pl.ds(f, nb, stride=half), :], out
            )
        return out

    def greet(semaphore, **place):
        pl.semaphore_signal(
            semaphore, inc=1, device_id=place, device_id_type=MESH
        )

    barrier = pltpu.get_barrier_semaphore()
    head, pair = space - 1, (space // 2 - 1, space // 2)
    inner = pair if exchange and space > 3 else ()

    for k in reversed(range(space)):
        @pl.when(z == k)
        def _():
            order = send_order(k, space, chunks) if exchange else []
            if k in inner:
                mate = sum(inner) - k
                greet(barrier, space=mate)
                greet(barrier, space=head)
                pl.semaphore_wait(barrier, 1)
                while order[0][1] == mate:
                    send(*order.pop(0)).start()
            elif k < head:
                greet(barrier, space=head)
            if k < head:
                pl.semaphore_wait(here, 1)
            elif k > 0:
                pl.semaphore_wait(barrier, head)
                for p in reversed(range(head)):
                    greet(here, space=p)
            for q, p in order:
                send(q, p).start()

    constants = [
        pltpu.make_async_copy(weight_in, weight, c_sem.at[0]),
        pltpu.make_async_copy(table_in, table, c_sem.at[1]),
    ]
    for copy in constants:
        copy.start()
    for q in range(chunks):
        local(q).start()

    @pl.when(z == 0)
    def _():
        for c, o in [*lines, (other, m)]:
            greet(barrier, freq=c, tm=o)
        pl.semaphore_wait(barrier, len(lines) + 1)
        for p in range(1, space):
            greet(ready, space=p)

    @pl.when(z > 0)
    def _():
        pl.semaphore_wait(ready, 1)

    for copy in constants:
        copy.wait()

    acc[...] = jnp.zeros_like(acc)
    step = GROUP * half

    @pl.loop(0, chunks)
    def _(q):
        wait(recv.at[q], s_recv.at[q])
        flat = [
            recv[q, :, b : b + GROUP].reshape(-1, width) for b in range(0, nb, GROUP)
        ]
        got = jnp.dot(
            table[...], jnp.concatenate(flat, axis=1),
            precision=HIGHEST, preferred_element_type=jnp.float32,
        )
        for c in range(2):
            for r in range(2):
                top = (c * 2 + r) * step
                for g in range(nb // GROUP):
                    spec[q, c, r, g * step : (g + 1) * step] = got[
                        top : top + step, g * width : (g + 1) * width
                    ]
        w = weight[core, q]
        for c in (other, core):
            re, im = spec[q, c, 0], spec[q, c, 1]
            left = jnp.concatenate([re * w, im * w], axis=1)
            right = jnp.concatenate([re + im, im - re], axis=1)
            acc[c] += lax.dot_general(
                left, right, (((1,), (1,)), ((), ())),
                precision=HIGHEST, preferred_element_type=jnp.float32,
            )
            if c is other:
                @pl.when(q == chunks - 1)
                def _():
                    g_side[0] = diagonal(other)
                    fold().start()

        @pl.when(q < chunks - 1)
        def _():
            trade(q).start()

    part = diagonal(core)
    fold().wait_recv()
    g_send[...] = part + g_side[1]
    for p in range(space):
        for _, o in lines:
            gram_copy(o, p).start()
        if p < space - 1:
            gram_copy(m, jnp.where(p < z, p, p + 1)).start()
    own = pltpu.make_async_copy(g_send, g_recv.at[mine], g_got)
    own.start()
    trade(chunks - 1).start()

    def put(ref, q, start):
        place = pl.ds(pl.multiple_of(start * rows + q * width, width), width)
        for r in range(2):
            for f in range(half):
                first, middle, last = split(ref[r, pl.ds(f, nb, stride=half), :])
                g, top = f // PACK, (r * PACK + f % PACK) * nb
                x_out[g, 0, top : top + nb, place] = first
                x_out[g, 1, top : top + nb, place] = middle
                low_out[g, top : top + nb, place] = last

    @pl.loop(0, chunks)
    def _(q):
        put(spec.at[q, core], q, core)

    wait(inbox, p_recv)

    @pl.loop(0, chunks)
    def _(q):
        put(inbox.at[q], q, other)

    wait(inbox, p_send)
    if exchange and space > 1:
        wait(recv.at[:, : space - 1], s_send)
    wait(g_recv, g_got)
    slots = [g_recv[s] for s in range(space * tm)]
    while len(slots) > 1:
        slots = [
            sum(slots[i + 1 : i + 2], slots[i]) for i in range(0, len(slots), 2)
        ]
    g_out[...] = slots[0] * (1.0 / total)
    fold().wait_send()
    if space * tm > 1:
        wait(g_recv.at[: space * tm - 1], g_sent)


def modes_kernel(half, gram, x, low, modes, upper, out, triangle, m_sem, u_sem):
    nb, lanes = gram.shape
    row = lax.broadcasted_iota(jnp.int32, (nb, lanes), 0)
    lane = lax.broadcasted_iota(jnp.int32, (nb, lanes), 1)
    col = lane % nb
    which = lane // nb

    def pick(a, index):
        return jnp.take_along_axis(a, index, axis=1, mode="promise_in_bounds")

    mixed = pick(gram[...], col * half + which)
    turned = mixed.T
    turned = jnp.concatenate(
        [turned[f * nb : (f + 1) * nb] for f in range(half)], axis=1
    )
    re = (mixed + turned) * 0.5 + jnp.where(row == col, epsilon, 0.0)
    im = (mixed - turned) * 0.5
    diag = jnp.zeros_like(re)
    for start in range(0, nb, PANEL):
        panel = []
        for p in range(start, start + PANEL):
            index = which * nb + p
            panel.append((pick(re, index), pick(im, index)))
        for p in range(start, start + PANEL):
            cr, ci = panel[p - start]
            diag = jnp.where(row == p, cr, diag)
            if p == nb - 1:
                break
            inv = 1.0 / cr[p : p + 1]
            mr, mi = cr * inv, ci * inv
            for k in range(p - start + 1, PANEL):
                kr, ki = panel[k]
                sr, si = kr[p : p + 1], ki[p : p + 1]
                panel[k] = kr - (mr * sr - mi * si), ki - (mr * si + mi * sr)
            pr, pi = re[p : p + 1], im[p : p + 1]
            here = col == p
            nr = jnp.where(here, 0.0, re) - (
                mr * jnp.where(here[:1], 1.0, pr) - mi * jnp.where(here[:1], 0.0, pi)
            )
            ni = jnp.where(here, 0.0, im) - (
                mr * jnp.where(here[:1], 0.0, pi) + mi * jnp.where(here[:1], 1.0, pr)
            )
            re = jnp.where(row > p, nr, re)
            im = jnp.where(row > p, ni, im)
    pivot = jnp.sqrt(diag)
    scale = 1.0 / pivot
    re, im = re * scale, im * scale
    lr = jnp.where(col < row, re, jnp.where(col == row, scale, 0.0))
    li = jnp.where(col < row, im, 0.0)
    left = lane < PACK * nb
    other_r = pltpu.roll(lr, PACK * nb, axis=1)
    other_i = pltpu.roll(li, PACK * nb, axis=1)
    tops = (
        (jnp.where(left, lr, other_i), jnp.where(left, -li, other_r)),
        (jnp.where(left, other_r, li), jnp.where(left, -other_i, lr)),
    )
    spot = which % PACK
    copies = []
    span = x.shape[-1] // 2
    for g in range(half // PACK):
        parts = [[], [], []]
        for k in range(PACK):
            for block in tops[g]:
                for level, term in zip(parts, split(jnp.where(spot == k, block, 0.0))):
                    level.append(term)
        first, middle, last = (jnp.concatenate(level, axis=0) for level in parts)
        stack = jnp.concatenate(
            [
                jnp.concatenate([first, first], axis=1),
                jnp.concatenate([middle, middle], axis=1),
                jnp.concatenate([last, jnp.zeros_like(last)], axis=1),
            ],
            axis=0,
        )
        n = first.shape[0]
        for c in range(2):
            place = pl.ds(c * span, span)
            high = x[g, :, :, place].reshape(2 * n, span)
            got = jnp.dot(stack, high, preferred_element_type=jnp.float32)
            small = jnp.dot(first, low[g, :, place], preferred_element_type=jnp.float32)
            total = got[:n] + (got[n : 2 * n] + (got[2 * n :] + small))
            out[g, :, :, :, place] = total.reshape(PACK, 2, nb, span)
            copies.append(
                pltpu.make_async_copy(
                    out.at[g, :, :, :, place],
                    modes.at[pl.ds(g * PACK, PACK), :, :, place],
                    m_sem.at[g, c],
                )
            )
            copies[-1].start()
        if g == 0:
            ur = jnp.where(col > row, re, jnp.where(col == row, pivot, 0.0))
            ui = jnp.where(col > row, im, 0.0)
            for f in range(half):
                triangle[0, f] = ur[:, f * nb : (f + 1) * nb]
                triangle[1, f] = ui[:, f * nb : (f + 1) * nb]
            copies.append(pltpu.make_async_copy(triangle, upper, u_sem))
            copies[-1].start()
    for copy in copies:
        copy.wait()


def modes_call(gram, x, low):
    nb, lanes = gram.shape
    half = lanes // nb
    columns = x.shape[-1]
    vmem = pl.BlockSpec(memory_space=pltpu.VMEM)
    hbm = pl.BlockSpec(memory_space=pltpu.HBM)
    dma = pltpu.SemaphoreType.DMA
    groups = half // PACK
    return pl.pallas_call(
        functools.partial(modes_kernel, half),
        out_shape=(
            jax.ShapeDtypeStruct((half, 2, nb, columns), jnp.float32),
            jax.ShapeDtypeStruct((2, half, nb, nb), jnp.float32),
        ),
        in_specs=[vmem, vmem, vmem],
        out_specs=(hbm, hbm),
        scratch_shapes=[
            pltpu.VMEM((groups, PACK, 2, nb, columns), jnp.float32),
            pltpu.VMEM((2, half, nb, nb), jnp.float32),
            dma((groups, 2)),
            dma,
        ],
        compiler_params=pltpu.CompilerParams(vmem_limit_bytes=40 * 2**20),
        name="modes",
    )(gram, x, low)


def in_hbm(a):
    return pltpu.with_memory_space_constraint(a, pltpu.HBM)


def on_device(snapshots, weights):
    freq = lax.axis_size("freq")
    space = lax.axis_size("space")
    tm = lax.axis_size("tm")
    assert freq == 2
    half = NF // freq
    nb, local_times, columns = snapshots.shape
    rows = columns // (space * freq)
    exchange = local_times % 8 == 0
    if not exchange:
        shaped = snapshots.reshape(nb, local_times, space, freq, rows)
        own = lax.dynamic_index_in_dim(shaped, lax.axis_index("freq"), 3, keepdims=False)
        pieces = lax.all_to_all(own, "space", split_axis=2, concat_axis=1, tiled=True)
        snapshots = pieces.reshape(nb, SEGMENT_FRAMES, rows)
    senders = space if exchange else 1
    times = SEGMENT_FRAMES // senders
    chunks = rows // min(rows, LANES)
    weight = weights.reshape(freq, chunks, 1, rows // chunks)
    table = jnp.asarray(dft_table(half, senders, times))
    lanes = nb * half
    vmem = pl.BlockSpec(memory_space=pltpu.VMEM)
    dma = pltpu.SemaphoreType.DMA
    x, low, gram = pl.pallas_call(
        functools.partial(
            spectra_kernel, exchange, space, tm, weights.shape[0] * space * tm
        ),
        out_shape=(
            pltpu.VMEM((half // PACK, 2, 2 * PACK * nb, freq * rows), jnp.bfloat16),
            pltpu.VMEM((half // PACK, 2 * PACK * nb, freq * rows), jnp.bfloat16),
            pltpu.VMEM((nb, lanes), jnp.float32),
        ),
        in_specs=[pl.BlockSpec(memory_space=pltpu.HBM)] * 3,
        out_specs=(vmem, vmem, vmem),
        scratch_shapes=[
            pltpu.VMEM(weight.shape, jnp.float32),
            pltpu.VMEM(table.shape, jnp.float32),
            pltpu.VMEM((chunks, senders, nb, times, rows // chunks), jnp.float32),
            pltpu.VMEM((chunks, freq, 2, lanes, rows // chunks), jnp.float32),
            pltpu.VMEM((chunks, 2, lanes, rows // chunks), jnp.float32),
            pltpu.VMEM((freq, lanes, lanes), jnp.float32),
            pltpu.VMEM((2, nb, lanes), jnp.float32),
            pltpu.VMEM((nb, lanes), jnp.float32),
            pltpu.VMEM((space * tm, nb, lanes), jnp.float32),
            dma((2,)),
            dma,
            dma((chunks,)),
            dma,
            dma,
            dma,
            dma,
            dma,
            dma,
            pltpu.SemaphoreType.REGULAR,
            pltpu.SemaphoreType.REGULAR,
        ],
        compiler_params=pltpu.CompilerParams(
            collective_id=0, has_side_effects=True, vmem_limit_bytes=52 * 2**20
        ),
        name="spectra",
    )(snapshots, in_hbm(weight), in_hbm(table))
    modes, upper = modes_call(gram, x, low)
    return modes, upper


def solution(mesh):
    return jax.shard_map(
        on_device,
        mesh=mesh,
        in_specs=(P(None, "space", ("groups", "tm")), P(("groups", "tm", "space"))),
        out_specs=(
            P("freq", None, None, ("groups", "tm", "space")),
            P("groups", "freq", None, None),
        ),
        check_vma=False,
    )
```

```python
import functools

import jax
import jax.numpy as jnp
import numpy as np
from jax import lax
from jax.experimental import pallas as pl
from jax.experimental.pallas import tpu as pltpu
from jax.sharding import PartitionSpec as P

SEGMENT_FRAMES = 64
NF = 16
GROUP = 8
LANES = 128
PACK = 4
PANEL = 8

epsilon = 1e-05
MESH = pl.DeviceIdType.MESH
HIGHEST = lax.Precision.HIGHEST


def dft_table(half, senders, local_times):
    moments = np.arange(SEGMENT_FRAMES)
    hann = 0.5 - 0.5 * np.cos(2.0 * np.pi * moments / SEGMENT_FRAMES)
    taper = hann / np.sqrt(np.sum(hann * hann))
    angle = (np.arange(NF) + 1)[:, None] * moments[None, :] % SEGMENT_FRAMES
    phase = 2.0 * np.pi * angle / SEGMENT_FRAMES
    pair = np.stack([np.cos(phase) * taper, -np.sin(phase) * taper])
    pair = pair.reshape(2, NF // half, half, senders, local_times)
    full = np.einsum("rhfzt,bc->hrbfzct", pair, np.eye(GROUP))
    shape = (2 * NF * GROUP, senders * GROUP * local_times)
    return full.reshape(shape).astype(np.float32)


def send_order(k, space, chunks):
    middle = space // 2
    halves = [p for p in range(middle)], [p for p in range(middle, space)]
    here, there = halves if k < middle else halves[::-1]
    cross = sorted(there, key=lambda p: -abs(p - k))
    near = [p for p in here if p != k]
    early, late = cross[:-1], cross[-1:]
    order = [(q, p) for p in late for q in range(2)]
    if k in (middle - 1, middle):
        order += [(q, p) for q in range(chunks) for p in early]
        order += [(q, p) for q in range(chunks) for p in near + late]
    else:
        order += [(q, p) for q in range(chunks) for p in early + near]
        order += [(q, p) for q in range(chunks) for p in late]
    return list(dict.fromkeys(order))


def split(a):
    first = a.astype(jnp.bfloat16)
    rest = a - first.astype(jnp.float32)
    middle = rest.astype(jnp.bfloat16)
    last = (rest - middle.astype(jnp.float32)).astype(jnp.bfloat16)
    return first, middle, last


def spectra_kernel(
    exchange, space, tm, total, snap, weight_in, table_in, x_out, low_out, g_out,
    weight, table, recv, spec, inbox, acc, g_side, g_send, g_recv,
    c_sem, s_send, s_recv, p_send, p_recv, g_sent, g_got, f_sent, f_got, here, ready,
):
    core = lax.axis_index("freq")
    z = lax.axis_index("space")
    m = lax.axis_index("tm")
    other = 1 - core
    chunks, nb, width = recv.shape[0], recv.shape[2], recv.shape[4]
    rows = chunks * width
    half = NF // 2
    n = nb * half
    lines = [(core, lax.rem(m + d, tm)) for d in range(1, tm)]
    mine = m * space + z

    def cols(q):
        return pl.ds(q * width, width)

    def source(p, q):
        start = (p * 2 + core) * rows + q * width
        return snap.at[:, :, pl.ds(pl.multiple_of(start, width), width)]

    def local(q):
        return pltpu.make_async_copy(
            source(z, q) if exchange else snap.at[:, :, cols(q)],
            recv.at[q, z if exchange else 0],
            s_recv.at[q],
        )

    def send(q, p):
        return pltpu.make_async_remote_copy(
            src_ref=source(p, q),
            dst_ref=recv.at[q, z],
            send_sem=s_send,
            recv_sem=s_recv.at[q],
            device_id={"space": p},
            device_id_type=MESH,
        )

    def wait(ref, semaphore):
        pltpu.make_async_copy(ref, ref, semaphore).wait()

    def trade(q):
        return pltpu.make_async_remote_copy(
            src_ref=spec.at[q, other],
            dst_ref=inbox.at[q],
            send_sem=p_send,
            recv_sem=p_recv,
            device_id={"freq": other},
            device_id_type=MESH,
        )

    def gram_copy(o, p):
        return pltpu.make_async_remote_copy(
            src_ref=g_send,
            dst_ref=g_recv.at[mine],
            send_sem=g_sent,
            recv_sem=g_got,
            device_id={"tm": o, "space": p},
            device_id_type=MESH,
        )

    def fold():
        return pltpu.make_async_remote_copy(
            src_ref=g_side.at[0],
            dst_ref=g_side.at[1],
            send_sem=f_sent,
            recv_sem=f_got,
            device_id={"freq": other},
            device_id_type=MESH,
        )

    lane = lax.broadcasted_iota(jnp.int32, (nb, n), 1)

    def diagonal(c):
        out = acc[c, pl.ds(0, nb, stride=half), :]
        for f in range(1, half):
            out = jnp.where(
                lane % half == f, acc[c, pl.ds(f, nb, stride=half), :], out
            )
        return out

    def greet(semaphore, **place):
        pl.semaphore_signal(
            semaphore, inc=1, device_id=place, device_id_type=MESH
        )

    barrier = pltpu.get_barrier_semaphore()
    head, pair = space - 1, (space // 2 - 1, space // 2)
    inner = pair if exchange and space > 3 else ()

    @pl.when(z < head)
    def _():
        greet(barrier, space=head)

    for k in reversed(range(space)):
        @pl.when(z == k)
        def _():
            order = send_order(k, space, chunks) if exchange else []
            if k in inner:
                mate = sum(inner) - k
                greet(barrier, space=mate)
                pl.semaphore_wait(barrier, 1)
                while order[0][1] == mate:
                    send(*order.pop(0)).start()
            if k < head:
                pl.semaphore_wait(here, 1)
            elif k > 0:
                pl.semaphore_wait(barrier, head)
                for p in reversed(range(head)):
                    greet(here, space=p)
            for q, p in order:
                send(q, p).start()

    constants = [
        pltpu.make_async_copy(weight_in, weight, c_sem.at[0]),
        pltpu.make_async_copy(table_in, table, c_sem.at[1]),
    ]
    for copy in constants:
        copy.start()
    for q in range(chunks):
        local(q).start()

    @pl.when(z == 0)
    def _():
        for c, o in [*lines, (other, m)]:
            greet(barrier, freq=c, tm=o)
        pl.semaphore_wait(barrier, len(lines) + 1)
        for p in range(1, space):
            greet(ready, space=p)

    @pl.when(z > 0)
    def _():
        pl.semaphore_wait(ready, 1)

    for copy in constants:
        copy.wait()

    acc[...] = jnp.zeros_like(acc)
    step = GROUP * half

    @pl.loop(0, chunks)
    def _(q):
        wait(recv.at[q], s_recv.at[q])
        flat = [
            recv[q, :, b : b + GROUP].reshape(-1, width) for b in range(0, nb, GROUP)
        ]
        got = jnp.dot(
            table[...], jnp.concatenate(flat, axis=1),
            precision=HIGHEST, preferred_element_type=jnp.float32,
        )
        for c in range(2):
            for r in range(2):
                top = (c * 2 + r) * step
                for g in range(nb // GROUP):
                    spec[q, c, r, g * step : (g + 1) * step] = got[
                        top : top + step, g * width : (g + 1) * width
                    ]
        w = weight[core, q]
        for c in (other, core):
            re, im = spec[q, c, 0], spec[q, c, 1]
            left = jnp.concatenate([re * w, im * w], axis=1)
            right = jnp.concatenate([re + im, im - re], axis=1)
            acc[c] += lax.dot_general(
                left, right, (((1,), (1,)), ((), ())),
                precision=HIGHEST, preferred_element_type=jnp.float32,
            )
            if c is other:
                @pl.when(q == chunks - 1)
                def _():
                    g_side[0] = diagonal(other)
                    fold().start()

        trade(q).start()

    part = diagonal(core)
    fold().wait_recv()
    g_send[...] = part + g_side[1]
    for p in range(space):
        for _, o in lines:
            gram_copy(o, p).start()
        if p < space - 1:
            gram_copy(m, jnp.where(p < z, p, p + 1)).start()
    own = pltpu.make_async_copy(g_send, g_recv.at[mine], g_got)
    own.start()

    def put(ref, q, start):
        place = pl.ds(pl.multiple_of(start * rows + q * width, width), width)
        for r in range(2):
            for f in range(half):
                first, middle, last = split(ref[r, pl.ds(f, nb, stride=half), :])
                g, top = f // PACK, (r * PACK + f % PACK) * nb
                x_out[g, 0, top : top + nb, place] = first
                x_out[g, 1, top : top + nb, place] = middle
                low_out[g, top : top + nb, place] = last

    @pl.loop(0, chunks)
    def _(q):
        put(spec.at[q, core], q, core)

    wait(inbox, p_recv)

    @pl.loop(0, chunks)
    def _(q):
        put(inbox.at[q], q, other)

    wait(inbox, p_send)
    if exchange and space > 1:
        wait(recv.at[:, : space - 1], s_send)
    wait(g_recv, g_got)
    slots = [g_recv[s] for s in range(space * tm)]
    while len(slots) > 1:
        slots = [
            sum(slots[i + 1 : i + 2], slots[i]) for i in range(0, len(slots), 2)
        ]
    g_out[...] = slots[0] * (1.0 / total)
    fold().wait_send()
    if space * tm > 1:
        wait(g_recv.at[: space * tm - 1], g_sent)


def modes_kernel(half, gram, x, low, modes, upper, out, triangle, m_sem, u_sem):
    nb, lanes = gram.shape
    row = lax.broadcasted_iota(jnp.int32, (nb, lanes), 0)
    lane = lax.broadcasted_iota(jnp.int32, (nb, lanes), 1)
    col = lane % nb
    which = lane // nb

    def pick(a, index):
        return jnp.take_along_axis(a, index, axis=1, mode="promise_in_bounds")

    mixed = pick(gram[...], col * half + which)
    turned = mixed.T
    turned = jnp.concatenate(
        [turned[f * nb : (f + 1) * nb] for f in range(half)], axis=1
    )
    re = (mixed + turned) * 0.5 + jnp.where(row == col, epsilon, 0.0)
    im = (mixed - turned) * 0.5
    diag = jnp.zeros_like(re)
    for start in range(0, nb, PANEL):
        panel = []
        for p in range(start, start + PANEL):
            index = which * nb + p
            panel.append((pick(re, index), pick(im, index)))
        for p in range(start, start + PANEL):
            cr, ci = panel[p - start]
            diag = jnp.where(row == p, cr, diag)
            if p == nb - 1:
                break
            inv = 1.0 / cr[p : p + 1]
            mr, mi = cr * inv, ci * inv
            for k in range(p - start + 1, PANEL):
                kr, ki = panel[k]
                sr, si = kr[p : p + 1], ki[p : p + 1]
                panel[k] = kr - (mr * sr - mi * si), ki - (mr * si + mi * sr)
            pr, pi = re[p : p + 1], im[p : p + 1]
            here = col == p
            nr = jnp.where(here, 0.0, re) - (
                mr * jnp.where(here[:1], 1.0, pr) - mi * jnp.where(here[:1], 0.0, pi)
            )
            ni = jnp.where(here, 0.0, im) - (
                mr * jnp.where(here[:1], 0.0, pi) + mi * jnp.where(here[:1], 1.0, pr)
            )
            re = jnp.where(row > p, nr, re)
            im = jnp.where(row > p, ni, im)
    pivot = jnp.sqrt(diag)
    scale = 1.0 / pivot
    re, im = re * scale, im * scale
    lr = jnp.where(col < row, re, jnp.where(col == row, scale, 0.0))
    li = jnp.where(col < row, im, 0.0)
    left = lane < PACK * nb
    other_r = pltpu.roll(lr, PACK * nb, axis=1)
    other_i = pltpu.roll(li, PACK * nb, axis=1)
    tops = (
        (jnp.where(left, lr, other_i), jnp.where(left, -li, other_r)),
        (jnp.where(left, other_r, li), jnp.where(left, -other_i, lr)),
    )
    spot = which % PACK
    copies = []
    span = x.shape[-1] // 2
    for g in range(half // PACK):
        parts = [[], [], []]
        for k in range(PACK):
            for block in tops[g]:
                for level, term in zip(parts, split(jnp.where(spot == k, block, 0.0))):
                    level.append(term)
        first, middle, last = (jnp.concatenate(level, axis=0) for level in parts)
        stack = jnp.concatenate(
            [
                jnp.concatenate([first, first], axis=1),
                jnp.concatenate([middle, middle], axis=1),
                jnp.concatenate([last, jnp.zeros_like(last)], axis=1),
            ],
            axis=0,
        )
        n = first.shape[0]
        for c in range(2):
            place = pl.ds(c * span, span)
            high = x[g, :, :, place].reshape(2 * n, span)
            got = jnp.dot(stack, high, preferred_element_type=jnp.float32)
            small = jnp.dot(first, low[g, :, place], preferred_element_type=jnp.float32)
            total = got[:n] + (got[n : 2 * n] + (got[2 * n :] + small))
            out[g, :, :, :, place] = total.reshape(PACK, 2, nb, span)
            copies.append(
                pltpu.make_async_copy(
                    out.at[g, :, :, :, place],
                    modes.at[pl.ds(g * PACK, PACK), :, :, place],
                    m_sem.at[g, c],
                )
            )
            copies[-1].start()
        if g == 0:
            ur = jnp.where(col > row, re, jnp.where(col == row, pivot, 0.0))
            ui = jnp.where(col > row, im, 0.0)
            for f in range(half):
                triangle[0, f] = ur[:, f * nb : (f + 1) * nb]
                triangle[1, f] = ui[:, f * nb : (f + 1) * nb]
            copies.append(pltpu.make_async_copy(triangle, upper, u_sem))
            copies[-1].start()
    for copy in copies:
        copy.wait()


def modes_call(gram, x, low):
    nb, lanes = gram.shape
    half = lanes // nb
    columns = x.shape[-1]
    vmem = pl.BlockSpec(memory_space=pltpu.VMEM)
    hbm = pl.BlockSpec(memory_space=pltpu.HBM)
    dma = pltpu.SemaphoreType.DMA
    groups = half // PACK
    return pl.pallas_call(
        functools.partial(modes_kernel, half),
        out_shape=(
            jax.ShapeDtypeStruct((half, 2, nb, columns), jnp.float32),
            jax.ShapeDtypeStruct((2, half, nb, nb), jnp.float32),
        ),
        in_specs=[vmem, vmem, vmem],
        out_specs=(hbm, hbm),
        scratch_shapes=[
            pltpu.VMEM((groups, PACK, 2, nb, columns), jnp.float32),
            pltpu.VMEM((2, half, nb, nb), jnp.float32),
            dma((groups, 2)),
            dma,
        ],
        compiler_params=pltpu.CompilerParams(vmem_limit_bytes=40 * 2**20),
        name="modes",
    )(gram, x, low)


def in_hbm(a):
    return pltpu.with_memory_space_constraint(a, pltpu.HBM)


def on_device(snapshots, weights):
    freq = lax.axis_size("freq")
    space = lax.axis_size("space")
    tm = lax.axis_size("tm")
    assert freq == 2
    half = NF // freq
    nb, local_times, columns = snapshots.shape
    rows = columns // (space * freq)
    exchange = local_times % 8 == 0
    if not exchange:
        shaped = snapshots.reshape(nb, local_times, space, freq, rows)
        own = lax.dynamic_index_in_dim(shaped, lax.axis_index("freq"), 3, keepdims=False)
        pieces = lax.all_to_all(own, "space", split_axis=2, concat_axis=1, tiled=True)
        snapshots = pieces.reshape(nb, SEGMENT_FRAMES, rows)
    senders = space if exchange else 1
    times = SEGMENT_FRAMES // senders
    chunks = rows // min(rows, LANES)
    weight = weights.reshape(freq, chunks, 1, rows // chunks)
    table = jnp.asarray(dft_table(half, senders, times))
    lanes = nb * half
    vmem = pl.BlockSpec(memory_space=pltpu.VMEM)
    dma = pltpu.SemaphoreType.DMA
    x, low, gram = pl.pallas_call(
        functools.partial(
            spectra_kernel, exchange, space, tm, weights.shape[0] * space * tm
        ),
        out_shape=(
            pltpu.VMEM((half // PACK, 2, 2 * PACK * nb, freq * rows), jnp.bfloat16),
            pltpu.VMEM((half // PACK, 2 * PACK * nb, freq * rows), jnp.bfloat16),
            pltpu.VMEM((nb, lanes), jnp.float32),
        ),
        in_specs=[pl.BlockSpec(memory_space=pltpu.HBM)] * 3,
        out_specs=(vmem, vmem, vmem),
        scratch_shapes=[
            pltpu.VMEM(weight.shape, jnp.float32),
            pltpu.VMEM(table.shape, jnp.float32),
            pltpu.VMEM((chunks, senders, nb, times, rows // chunks), jnp.float32),
            pltpu.VMEM((chunks, freq, 2, lanes, rows // chunks), jnp.float32),
            pltpu.VMEM((chunks, 2, lanes, rows // chunks), jnp.float32),
            pltpu.VMEM((freq, lanes, lanes), jnp.float32),
            pltpu.VMEM((2, nb, lanes), jnp.float32),
            pltpu.VMEM((nb, lanes), jnp.float32),
            pltpu.VMEM((space * tm, nb, lanes), jnp.float32),
            dma((2,)),
            dma,
            dma((chunks,)),
            dma,
            dma,
            dma,
            dma,
            dma,
            dma,
            pltpu.SemaphoreType.REGULAR,
            pltpu.SemaphoreType.REGULAR,
        ],
        compiler_params=pltpu.CompilerParams(
            collective_id=0, has_side_effects=True, vmem_limit_bytes=52 * 2**20
        ),
        name="spectra",
    )(snapshots, in_hbm(weight), in_hbm(table))
    modes, upper = modes_call(gram, x, low)
    return modes, upper


def solution(mesh):
    return jax.shard_map(
        on_device,
        mesh=mesh,
        in_specs=(P(None, "space", ("groups", "tm")), P(("groups", "tm", "space"))),
        out_specs=(
            P("freq", None, None, ("groups", "tm", "space")),
            P("groups", "freq", None, None),
        ),
        check_vma=False,
    )
```

```python
import functools

import jax
import jax.numpy as jnp
import numpy as np
from jax import lax
from jax.experimental import pallas as pl
from jax.experimental.pallas import tpu as pltpu
from jax.sharding import PartitionSpec as P

SEGMENT_FRAMES = 64
NF = 16
GROUP = 8
LANES = 128
PACK = 4
PANEL = 8

epsilon = 1e-05
MESH = pl.DeviceIdType.MESH
HIGHEST = lax.Precision.HIGHEST


def dft_table(half, senders, local_times):
    moments = np.arange(SEGMENT_FRAMES)
    hann = 0.5 - 0.5 * np.cos(2.0 * np.pi * moments / SEGMENT_FRAMES)
    taper = hann / np.sqrt(np.sum(hann * hann))
    angle = (np.arange(NF) + 1)[:, None] * moments[None, :] % SEGMENT_FRAMES
    phase = 2.0 * np.pi * angle / SEGMENT_FRAMES
    pair = np.stack([np.cos(phase) * taper, -np.sin(phase) * taper])
    pair = pair.reshape(2, NF // half, half, senders, local_times)
    full = np.einsum("rhfzt,bc->hrbfzct", pair, np.eye(GROUP))
    shape = (2 * NF * GROUP, senders * GROUP * local_times)
    return full.reshape(shape).astype(np.float32)


def send_order(k, space, chunks):
    middle = space // 2
    halves = [p for p in range(middle)], [p for p in range(middle, space)]
    here, there = halves if k < middle else halves[::-1]
    cross = sorted(there, key=lambda p: -abs(p - k))
    near = [p for p in here if p != k]
    early, late = cross[:-1], cross[-1:]
    order = [(q, p) for p in late for q in range(2)]
    if k in (middle - 1, middle):
        order += [(q, p) for q in range(chunks) for p in early]
        order += [(q, p) for q in range(chunks) for p in near + late]
    else:
        order += [(q, p) for q in range(chunks) for p in early + near]
        order += [(q, p) for q in range(chunks) for p in late]
    return list(dict.fromkeys(order))


def split(a):
    first = a.astype(jnp.bfloat16)
    rest = a - first.astype(jnp.float32)
    middle = rest.astype(jnp.bfloat16)
    last = (rest - middle.astype(jnp.float32)).astype(jnp.bfloat16)
    return first, middle, last


def spectra_kernel(
    exchange, space, tm, total, snap, weight_in, table_in, x_out, low_out, g_out,
    weight, table, recv, spec, inbox, acc, g_side, g_send, g_recv,
    c_sem, s_send, s_recv, p_send, p_recv, g_sent, g_got, f_sent, f_got, here, ready,
):
    core = lax.axis_index("freq")
    z = lax.axis_index("space")
    m = lax.axis_index("tm")
    other = 1 - core
    chunks, nb, width = recv.shape[0], recv.shape[2], recv.shape[4]
    rows = chunks * width
    half = NF // 2
    n = nb * half
    lines = [(core, lax.rem(m + d, tm)) for d in range(1, tm)]
    mine = m * space + z

    def cols(q):
        return pl.ds(q * width, width)

    def source(p, q):
        start = (p * 2 + core) * rows + q * width
        return snap.at[:, :, pl.ds(pl.multiple_of(start, width), width)]

    def local(q):
        return pltpu.make_async_copy(
            source(z, q) if exchange else snap.at[:, :, cols(q)],
            recv.at[q, z if exchange else 0],
            s_recv.at[q],
        )

    def send(q, p):
        return pltpu.make_async_remote_copy(
            src_ref=source(p, q),
            dst_ref=recv.at[q, z],
            send_sem=s_send,
            recv_sem=s_recv.at[q],
            device_id={"space": p},
            device_id_type=MESH,
        )

    def wait(ref, semaphore):
        pltpu.make_async_copy(ref, ref, semaphore).wait()

    def trade(q):
        return pltpu.make_async_remote_copy(
            src_ref=spec.at[q, other],
            dst_ref=inbox.at[q],
            send_sem=p_send,
            recv_sem=p_recv,
            device_id={"freq": other},
            device_id_type=MESH,
        )

    def gram_copy(o, p):
        return pltpu.make_async_remote_copy(
            src_ref=g_send,
            dst_ref=g_recv.at[mine],
            send_sem=g_sent,
            recv_sem=g_got,
            device_id={"tm": o, "space": p},
            device_id_type=MESH,
        )

    def fold():
        return pltpu.make_async_remote_copy(
            src_ref=g_side.at[0],
            dst_ref=g_side.at[1],
            send_sem=f_sent,
            recv_sem=f_got,
            device_id={"freq": other},
            device_id_type=MESH,
        )

    lane = lax.broadcasted_iota(jnp.int32, (nb, n), 1)

    def diagonal(c):
        out = acc[c, pl.ds(0, nb, stride=half), :]
        for f in range(1, half):
            out = jnp.where(
                lane % half == f, acc[c, pl.ds(f, nb, stride=half), :], out
            )
        return out

    def greet(semaphore, **place):
        pl.semaphore_signal(
            semaphore, inc=1, device_id=place, device_id_type=MESH
        )

    constants = [
        pltpu.make_async_copy(weight_in, weight, c_sem.at[0]),
        pltpu.make_async_copy(table_in, table, c_sem.at[1]),
    ]

    def begin():
        for copy in constants:
            copy.start()
        for q in range(chunks):
            local(q).start()

    barrier = pltpu.get_barrier_semaphore()
    head, pair = space - 1, (space // 2 - 1, space // 2)
    inner = pair if exchange and space > 3 else ()

    for k in reversed(range(space)):
        @pl.when(z == k)
        def _():
            order = send_order(k, space, chunks) if exchange else []
            if k in inner:
                mate = sum(inner) - k
                greet(barrier, space=mate)
                greet(barrier, space=head)
                begin()
                pl.semaphore_wait(barrier, 1)
                while order[0][1] == mate:
                    send(*order.pop(0)).start()
            else:
                if k < head:
                    greet(barrier, space=head)
                begin()
            if k < head:
                pl.semaphore_wait(here, 1)
            elif k > 0:
                pl.semaphore_wait(barrier, head)
                for p in reversed(range(head)):
                    greet(here, space=p)
            for q, p in order:
                send(q, p).start()

    @pl.when(z == 0)
    def _():
        for c, o in [*lines, (other, m)]:
            greet(barrier, freq=c, tm=o)
        pl.semaphore_wait(barrier, len(lines) + 1)
        for p in range(1, space):
            greet(ready, space=p)

    @pl.when(z > 0)
    def _():
        pl.semaphore_wait(ready, 1)

    for copy in constants:
        copy.wait()

    acc[...] = jnp.zeros_like(acc)
    step = GROUP * half

    @pl.loop(0, chunks)
    def _(q):
        wait(recv.at[q], s_recv.at[q])
        flat = [
            recv[q, :, b : b + GROUP].reshape(-1, width) for b in range(0, nb, GROUP)
        ]
        got = jnp.dot(
            table[...], jnp.concatenate(flat, axis=1),
            precision=HIGHEST, preferred_element_type=jnp.float32,
        )
        for c in range(2):
            for r in range(2):
                top = (c * 2 + r) * step
                for g in range(nb // GROUP):
                    spec[q, c, r, g * step : (g + 1) * step] = got[
                        top : top + step, g * width : (g + 1) * width
                    ]
        w = weight[core, q]
        for c in (other, core):
            re, im = spec[q, c, 0], spec[q, c, 1]
            left = jnp.concatenate([re * w, im * w], axis=1)
            right = jnp.concatenate([re + im, im - re], axis=1)
            acc[c] += lax.dot_general(
                left, right, (((1,), (1,)), ((), ())),
                precision=HIGHEST, preferred_element_type=jnp.float32,
            )
            if c is other:
                @pl.when(q == chunks - 1)
                def _():
                    g_side[0] = diagonal(other)
                    fold().start()

        @pl.when(q < chunks - 1)
        def _():
            trade(q).start()

    part = diagonal(core)
    fold().wait_recv()
    g_send[...] = part + g_side[1]
    for p in range(space):
        for _, o in lines:
            gram_copy(o, p).start()
        if p < space - 1:
            gram_copy(m, jnp.where(p < z, p, p + 1)).start()
    own = pltpu.make_async_copy(g_send, g_recv.at[mine], g_got)
    own.start()
    trade(chunks - 1).start()

    def put(ref, q, start):
        place = pl.ds(pl.multiple_of(start * rows + q * width, width), width)
        for r in range(2):
            for f in range(half):
                first, middle, last = split(ref[r, pl.ds(f, nb, stride=half), :])
                g, top = f // PACK, (r * PACK + f % PACK) * nb
                x_out[g, 0, top : top + nb, place] = first
                x_out[g, 1, top : top + nb, place] = middle
                low_out[g, top : top + nb, place] = last

    @pl.loop(0, chunks)
    def _(q):
        put(spec.at[q, core], q, core)

    wait(inbox, p_recv)

    @pl.loop(0, chunks)
    def _(q):
        put(inbox.at[q], q, other)

    wait(inbox, p_send)
    if exchange and space > 1:
        wait(recv.at[:, : space - 1], s_send)
    wait(g_recv, g_got)
    slots = [g_recv[s] for s in range(space * tm)]
    while len(slots) > 1:
        slots = [
            sum(slots[i + 1 : i + 2], slots[i]) for i in range(0, len(slots), 2)
        ]
    g_out[...] = slots[0] * (1.0 / total)
    fold().wait_send()
    if space * tm > 1:
        wait(g_recv.at[: space * tm - 1], g_sent)


def modes_kernel(half, gram, x, low, modes, upper, out, triangle, m_sem, u_sem):
    nb, lanes = gram.shape
    row = lax.broadcasted_iota(jnp.int32, (nb, lanes), 0)
    lane = lax.broadcasted_iota(jnp.int32, (nb, lanes), 1)
    col = lane % nb
    which = lane // nb

    def pick(a, index):
        return jnp.take_along_axis(a, index, axis=1, mode="promise_in_bounds")

    mixed = pick(gram[...], col * half + which)
    turned = mixed.T
    turned = jnp.concatenate(
        [turned[f * nb : (f + 1) * nb] for f in range(half)], axis=1
    )
    re = (mixed + turned) * 0.5 + jnp.where(row == col, epsilon, 0.0)
    im = (mixed - turned) * 0.5
    diag = jnp.zeros_like(re)
    for start in range(0, nb, PANEL):
        panel = []
        for p in range(start, start + PANEL):
            index = which * nb + p
            panel.append((pick(re, index), pick(im, index)))
        for p in range(start, start + PANEL):
            cr, ci = panel[p - start]
            diag = jnp.where(row == p, cr, diag)
            if p == nb - 1:
                break
            inv = 1.0 / cr[p : p + 1]
            mr, mi = cr * inv, ci * inv
            for k in range(p - start + 1, PANEL):
                kr, ki = panel[k]
                sr, si = kr[p : p + 1], ki[p : p + 1]
                panel[k] = kr - (mr * sr - mi * si), ki - (mr * si + mi * sr)
            pr, pi = re[p : p + 1], im[p : p + 1]
            here = col == p
            nr = jnp.where(here, 0.0, re) - (
                mr * jnp.where(here[:1], 1.0, pr) - mi * jnp.where(here[:1], 0.0, pi)
            )
            ni = jnp.where(here, 0.0, im) - (
                mr * jnp.where(here[:1], 0.0, pi) + mi * jnp.where(here[:1], 1.0, pr)
            )
            re = jnp.where(row > p, nr, re)
            im = jnp.where(row > p, ni, im)
    pivot = jnp.sqrt(diag)
    scale = 1.0 / pivot
    re, im = re * scale, im * scale
    lr = jnp.where(col < row, re, jnp.where(col == row, scale, 0.0))
    li = jnp.where(col < row, im, 0.0)
    left = lane < PACK * nb
    other_r = pltpu.roll(lr, PACK * nb, axis=1)
    other_i = pltpu.roll(li, PACK * nb, axis=1)
    tops = (
        (jnp.where(left, lr, other_i), jnp.where(left, -li, other_r)),
        (jnp.where(left, other_r, li), jnp.where(left, -other_i, lr)),
    )
    spot = which % PACK
    copies = []
    span = x.shape[-1] // 2
    for g in range(half // PACK):
        parts = [[], [], []]
        for k in range(PACK):
            for block in tops[g]:
                for level, term in zip(parts, split(jnp.where(spot == k, block, 0.0))):
                    level.append(term)
        first, middle, last = (jnp.concatenate(level, axis=0) for level in parts)
        stack = jnp.concatenate(
            [
                jnp.concatenate([first, first], axis=1),
                jnp.concatenate([middle, middle], axis=1),
                jnp.concatenate([last, jnp.zeros_like(last)], axis=1),
            ],
            axis=0,
        )
        n = first.shape[0]
        for c in range(2):
            place = pl.ds(c * span, span)
            high = x[g, :, :, place].reshape(2 * n, span)
            got = jnp.dot(stack, high, preferred_element_type=jnp.float32)
            small = jnp.dot(first, low[g, :, place], preferred_element_type=jnp.float32)
            total = got[:n] + (got[n : 2 * n] + (got[2 * n :] + small))
            out[g, :, :, :, place] = total.reshape(PACK, 2, nb, span)
            copies.append(
                pltpu.make_async_copy(
                    out.at[g, :, :, :, place],
                    modes.at[pl.ds(g * PACK, PACK), :, :, place],
                    m_sem.at[g, c],
                )
            )
            copies[-1].start()
        if g == 0:
            ur = jnp.where(col > row, re, jnp.where(col == row, pivot, 0.0))
            ui = jnp.where(col > row, im, 0.0)
            for f in range(half):
                triangle[0, f] = ur[:, f * nb : (f + 1) * nb]
                triangle[1, f] = ui[:, f * nb : (f + 1) * nb]
            copies.append(pltpu.make_async_copy(triangle, upper, u_sem))
            copies[-1].start()
    for copy in copies:
        copy.wait()


def modes_call(gram, x, low):
    nb, lanes = gram.shape
    half = lanes // nb
    columns = x.shape[-1]
    vmem = pl.BlockSpec(memory_space=pltpu.VMEM)
    hbm = pl.BlockSpec(memory_space=pltpu.HBM)
    dma = pltpu.SemaphoreType.DMA
    groups = half // PACK
    return pl.pallas_call(
        functools.partial(modes_kernel, half),
        out_shape=(
            jax.ShapeDtypeStruct((half, 2, nb, columns), jnp.float32),
            jax.ShapeDtypeStruct((2, half, nb, nb), jnp.float32),
        ),
        in_specs=[vmem, vmem, vmem],
        out_specs=(hbm, hbm),
        scratch_shapes=[
            pltpu.VMEM((groups, PACK, 2, nb, columns), jnp.float32),
            pltpu.VMEM((2, half, nb, nb), jnp.float32),
            dma((groups, 2)),
            dma,
        ],
        compiler_params=pltpu.CompilerParams(vmem_limit_bytes=40 * 2**20),
        name="modes",
    )(gram, x, low)


def in_hbm(a):
    return pltpu.with_memory_space_constraint(a, pltpu.HBM)


def on_device(snapshots, weights):
    freq = lax.axis_size("freq")
    space = lax.axis_size("space")
    tm = lax.axis_size("tm")
    assert freq == 2
    half = NF // freq
    nb, local_times, columns = snapshots.shape
    rows = columns // (space * freq)
    exchange = local_times % 8 == 0
    if not exchange:
        shaped = snapshots.reshape(nb, local_times, space, freq, rows)
        own = lax.dynamic_index_in_dim(shaped, lax.axis_index("freq"), 3, keepdims=False)
        pieces = lax.all_to_all(own, "space", split_axis=2, concat_axis=1, tiled=True)
        snapshots = pieces.reshape(nb, SEGMENT_FRAMES, rows)
    senders = space if exchange else 1
    times = SEGMENT_FRAMES // senders
    chunks = rows // min(rows, LANES)
    weight = weights.reshape(freq, chunks, 1, rows // chunks)
    table = jnp.asarray(dft_table(half, senders, times))
    lanes = nb * half
    vmem = pl.BlockSpec(memory_space=pltpu.VMEM)
    dma = pltpu.SemaphoreType.DMA
    x, low, gram = pl.pallas_call(
        functools.partial(
            spectra_kernel, exchange, space, tm, weights.shape[0] * space * tm
        ),
        out_shape=(
            pltpu.VMEM((half // PACK, 2, 2 * PACK * nb, freq * rows), jnp.bfloat16),
            pltpu.VMEM((half // PACK, 2 * PACK * nb, freq * rows), jnp.bfloat16),
            pltpu.VMEM((nb, lanes), jnp.float32),
        ),
        in_specs=[pl.BlockSpec(memory_space=pltpu.HBM)] * 3,
        out_specs=(vmem, vmem, vmem),
        scratch_shapes=[
            pltpu.VMEM(weight.shape, jnp.float32),
            pltpu.VMEM(table.shape, jnp.float32),
            pltpu.VMEM((chunks, senders, nb, times, rows // chunks), jnp.float32),
            pltpu.VMEM((chunks, freq, 2, lanes, rows // chunks), jnp.float32),
            pltpu.VMEM((chunks, 2, lanes, rows // chunks), jnp.float32),
            pltpu.VMEM((freq, lanes, lanes), jnp.float32),
            pltpu.VMEM((2, nb, lanes), jnp.float32),
            pltpu.VMEM((nb, lanes), jnp.float32),
            pltpu.VMEM((space * tm, nb, lanes), jnp.float32),
            dma((2,)),
            dma,
            dma((chunks,)),
            dma,
            dma,
            dma,
            dma,
            dma,
            dma,
            pltpu.SemaphoreType.REGULAR,
            pltpu.SemaphoreType.REGULAR,
        ],
        compiler_params=pltpu.CompilerParams(
            collective_id=0, has_side_effects=True, vmem_limit_bytes=52 * 2**20
        ),
        name="spectra",
    )(snapshots, in_hbm(weight), in_hbm(table))
    modes, upper = modes_call(gram, x, low)
    return modes, upper


def solution(mesh):
    return jax.shard_map(
        on_device,
        mesh=mesh,
        in_specs=(P(None, "space", ("groups", "tm")), P(("groups", "tm", "space"))),
        out_specs=(
            P("freq", None, None, ("groups", "tm", "space")),
            P("groups", "freq", None, None),
        ),
        check_vma=False,
    )
```
